32 devices in a mesh: video: 2 (over y), rows: 4 (over z), cols: 4 (over x, core).
Axes of the slice: x: 2, y: 2, z: 4, core: 2. Of those that a mesh axis runs over, the one named last changes fastest.
Arguments:
- frame_in: bfloat16 [64, 80, 512], P(('video', 'rows'), 'cols'), parts along dimension 0, may hold values from -6 to 6
- norm_gain: float32 [512], replicated, may hold values from 0.5 to 1.5
- w_query: bfloat16 [512, 512], replicated, may hold values from -2 to 2
- w_key: bfloat16 [512, 512], replicated, may hold values from -0.125 to 0.125
- w_value: bfloat16 [512, 512], replicated, may hold values from -0.25 to 0.25
- w_out: bfloat16 [512, 512], replicated, may hold values from -0.25 to 0.25
- conv_gain: float32 [512], replicated, may hold values from 0.5 to 1.5
- conv_cache: bfloat16 [2, 64, 80, 512], P(None, ('video', 'rows'), 'cols'), parts along dimension 1, may hold values from -6 to 6
- w_conv: bfloat16 [3, 3, 3, 512, 256], replicated, may hold values from -0.0546875 to 0.0546875
- conv_bias: float32 [256], replicated, may hold values from -0.5 to 0.5
Outputs:
- hidden: bfloat16 [64, 80, 512], P(('video', 'rows'), 'cols'), parts along dimension 0
- mixed_out: bfloat16 [64, 80, 256], P(('video', 'rows'), 'cols'), parts along dimension 0
The draws below stay inside these ranges and needn't reach their ends.
There are 2 independent parts, one for each index of `video`. The reference program is written for one: setup_inputs(seed, part) draws one part's arguments, and reference() takes and returns one part's arrays. A program takes and returns all parts, laid end to end along the dimension named above; an argument that names none is the same for every part. Nothing has to cross between parts.
All inputs are finite; a program needn't handle non-finite values.
Results may differ from the reference program's by a relative error of at most 0.012.
Values may be sent and summed in bfloat16 or wider, within the bound.
No kernel may reach another device: no remote copies, remote signals or barrier semaphores. Data moves between devices by JAX's collectives and lax.ppermute only.
A program may use at most 128 MiB of HBM per device.

```python
import math
import jax
import jax.numpy as jnp
from jax import lax

C = 512
CO = 256
H = 32
W = 80


def weight_bases(key):
    inner = jax.random.fold_in(key, 4711)
    first_key, second_key = jax.random.split(inner)
    shared = jax.random.normal(first_key, (C, C), jnp.float32)
    others = jax.random.normal(second_key, (C, C), jnp.float32)
    return (shared, others)


def draw_w_key(key, part):
    shared, others = weight_bases(key)
    return jnp.clip(shared * (1.0 / math.sqrt(C)), -0.125, 0.125).astype(jnp.bfloat16)


def draw_w_query(key, part):
    shared, others = weight_bases(key)
    mixed_vals = jnp.clip(others * (1.0 / math.sqrt(C)), -0.125, 0.125)
    return mixed_vals.astype(jnp.bfloat16)


def draw_frame_in(key, part):
    base_key = jax.random.fold_in(key, 0)
    base = jnp.clip(jax.random.normal(base_key, (H, W, C), jnp.float32), -6.0, 6.0)
    return base.astype(jnp.bfloat16)


def level_of(rng, extent, shards, low, top_value):
    def one(dim, parts):
        heights = jax.random.uniform(jax.random.fold_in(jax.random.fold_in(rng, 6), dim), (parts,), jnp.float32, low / len(shards), top_value / len(shards))
        return jnp.repeat(jnp.exp(heights), extent[dim] // parts).reshape((-1,) + (1,) * (len(extent) - dim - 1))

    level = one(*shards[0])
    for cut in shards[1:]:
        level = level * one(*cut)
    return level


def bell_draw(own_key, dims, spread, most, shards=(), dtype=jnp.bfloat16):
    result = spread * jax.random.normal(own_key, dims, jnp.float32)
    if shards:
        result = result * level_of(own_key, dims, shards, -0.22, 0.18)
    return jnp.clip(result, -most, most).astype(dtype)


def setup_inputs(seed: int = 0, part: int = 0) -> dict:
    key_list = jax.random.split(jax.random.key(seed), 11)
    part_keys = jax.random.split(jax.random.fold_in(key_list[10], part), 11)
    return {
        "frame_in": draw_frame_in(jax.random.fold_in(jax.random.fold_in(key_list[10], part), 71), part),
        "norm_gain": jnp.clip(jax.random.uniform(key_list[1], (C,), jnp.float32, 0.5, 1.5), 0.5, 1.5),
        "w_query": draw_w_query(jax.random.fold_in(key_list[10], 71), part),
        "w_key": draw_w_key(jax.random.fold_in(key_list[10], 71), part),
        "w_value": bell_draw(key_list[4], (C, C), C ** -0.5, 0.25),
        "w_out": bell_draw(key_list[5], (C, C), C ** -0.5, 0.25),
        "conv_gain": jnp.clip(jax.random.uniform(key_list[6], (C,), jnp.float32, 0.5, 1.5), 0.5, 1.5),
        "conv_cache": bell_draw(part_keys[7], (2, H, W, C), 1.0, 6.0, ((1, 4), (2, 4))),
        "w_conv": bell_draw(key_list[8], (3, 3, 3, C, CO), (27 * C) ** -0.5, 0.0546875),
        "conv_bias": jnp.clip(jax.random.uniform(key_list[9], (CO,), jnp.float32, -0.5, 0.5), -0.5, 0.5),
    }


def rms_scaled(values, gain):
    mean_sq = lax.optimization_barrier(jnp.mean(values * values, axis=-1, keepdims=True))
    return values * lax.rsqrt(mean_sq + 1e-06) * gain

def reference(frame_in, norm_gain, w_query, w_key, w_value, w_out, conv_gain, conv_cache, w_conv, conv_bias):
    tokens = frame_in.astype(jnp.float32).reshape(H * W, C)
    normed = rms_scaled(tokens, norm_gain).astype(jnp.bfloat16)
    query_rows = (jnp.dot(normed, w_query, preferred_element_type=jnp.float32) * (1.0 / math.sqrt(C))).astype(jnp.bfloat16)
    query_keys = jnp.dot(query_rows, w_key.T, preferred_element_type=jnp.float32).astype(jnp.bfloat16)

    def one_row(query_block):
        scores = jnp.dot(query_block, normed.T, preferred_element_type=jnp.float32)
        peak = lax.optimization_barrier(jnp.max(scores, axis=1, keepdims=True))
        weights = jnp.exp(scores - peak)
        total_sum = lax.optimization_barrier(jnp.sum(weights, axis=1, keepdims=True))
        summed = jnp.dot(weights.astype(jnp.bfloat16), normed, preferred_element_type=jnp.float32)
        return (summed / total_sum).astype(jnp.bfloat16)
    pooled = lax.map(one_row, query_keys.reshape(H, W, C)).reshape(H * W, C)
    attended = jnp.dot(pooled, w_value, preferred_element_type=jnp.float32).astype(jnp.bfloat16)
    hidden = (tokens + jnp.dot(attended, w_out, preferred_element_type=jnp.float32)).astype(jnp.bfloat16)
    conv_input = jax.nn.silu(rms_scaled(hidden.astype(jnp.float32), conv_gain)).astype(jnp.bfloat16)
    stacked = jnp.concatenate([conv_cache, conv_input.reshape(1, H, W, C)], axis=0)
    padded = jnp.pad(stacked, ((0, 0), (1, 1), (1, 1), (0, 0)))
    result_sum = hidden[:, :CO].astype(jnp.float32) + conv_bias
    for time_off in range(3):
        for row_off in range(3):
            for col_off in range(3):
                window = padded[time_off, row_off:row_off + H, col_off:col_off + W, :].reshape(H * W, C)
                result_sum = result_sum + jnp.dot(window, w_conv[time_off, row_off, col_off], preferred_element_type=jnp.float32)
    return (hidden.reshape(H, W, C), result_sum.astype(jnp.bfloat16).reshape(H, W, CO))
```

```python
import functools
import math

import jax
import jax.numpy as jnp
from jax import lax
from jax.experimental import pallas as pl
from jax.experimental.pallas import tpu as pltpu
from jax.sharding import PartitionSpec as P

EPS = 1e-06
AXES = ("rows", "cols")
F32 = jnp.float32
BF16 = jnp.bfloat16
VM = pl.BlockSpec(memory_space=pltpu.VMEM)


def chip_cycle(height, width):
    if width == 1 or height == 1:
        return [(z, x) for z in range(height) for x in range(width)]
    order = []
    for x in range(width):
        inner = range(1, height) if x % 2 == 0 else range(height - 1, 0, -1)
        order += [(z, x) for z in inner]
    return order + [(0, x) for x in range(width - 1, -1, -1)]


def permutations(rows, cols):
    def at(z, x, core):
        return z * cols + 2 * x + core

    walk = chip_cycle(rows, cols // 2)
    ring = []
    for k, here in enumerate(walk):
        there = walk[(k + 1) % len(walk)]
        ring += [(at(*here, 0), at(*there, 0)), (at(*there, 1), at(*here, 1))]
    twin = [(i, i ^ 1) for i in range(rows * cols)]
    down = [(i, i + cols) for i in range((rows - 1) * cols)]
    up = [(j, i) for i, j in down]
    cross = []
    for r in range(rows):
        for c in range(1, cols - 1, 2):
            i = r * cols + c
            cross += [(i, i + 1), (i + 1, i)]
    return len(walk), ring, twin, down, up, cross


def edge_slots(width):
    return -(-(width + 2) // 16) * 16


def side_slots(height):
    return height + 8


def rms_scaled(values, gain):
    mean_sq = jnp.mean(values * values, axis=-1, keepdims=True)
    return values * lax.rsqrt(mean_sq + EPS) * gain


def dot(a, b):
    return jnp.dot(a, b, preferred_element_type=F32)


def dot_t(a, b):
    return lax.dot_general(a, b, (((1,), (1,)), ((), ())), preferred_element_type=F32)


def pack_rows_kernel(frame_ref, cache_ref, first_ref, last_ref):
    width, height, channels = frame_ref.shape
    fill = jnp.zeros((edge_slots(width) - width, channels), F32)
    for t in range(3):
        tile = (frame_ref[...] if t == 2 else cache_ref[t]).astype(F32)
        for r, out in ((0, first_ref), (height - 1, last_ref)):
            row = jnp.concatenate([tile[c, r : r + 1, :] for c in range(width)] + [fill], axis=0)
            out[t] = row.astype(BF16)


def pack_cols_kernel(frame_ref, cache_ref, top_ref, bottom_ref, twin_ref, cross_ref):
    width, height, channels = frame_ref.shape
    odd = lax.rem(lax.axis_index("cols"), 2)
    fill = jnp.zeros((side_slots(height) - height - 2, channels), F32)
    for t in range(3):
        sides = []
        for c in (0, width - 1):
            own = (frame_ref[c] if t == 2 else cache_ref[t, c]).astype(F32)
            top = top_ref[t].astype(F32)[c : c + 1, :]
            bottom = bottom_ref[t].astype(F32)[c : c + 1, :]
            sides.append(jnp.concatenate([own, top, bottom, fill], axis=0))
        left, right = sides
        twin_ref[t] = jnp.where(odd == 1, left, right).astype(BF16)
        cross_ref[t] = jnp.where(odd == 1, right, left).astype(BF16)


def extended(own, top, bottom, twin, cross, odd):
    height = twin.shape[0] - side_slots(0)
    left = jnp.where(odd == 1, twin, cross)
    right = jnp.where(odd == 1, cross, twin)
    slot = lax.broadcasted_iota(jnp.int32, top.shape, 0)
    width = own.shape[0] // height

    def edge(row, k):
        row = jnp.where(slot == width, right[k : k + 1, :], row)
        return jnp.where(slot == top.shape[0] - 1, left[k : k + 1, :], row)

    return jnp.concatenate(
        [edge(top, height), left[:height], own, right[:height], edge(bottom, height + 1)], axis=0
    )


def conv_rows(ext_len, slots, i):
    return (0 if i == 0 else slots), (ext_len if i == 2 else ext_len - slots)


def add_taps(sums, products, i, j, height, count):
    slots = edge_slots(count // height)
    main = products[slots:] if i == 0 else products
    part = main[j * height : j * height + count]
    edge = None
    if i == 0:
        edge = products[:slots]
    if i == 2:
        edge = products[products.shape[0] - slots :]
    if edge is not None and j != 1:
        edge = pltpu.roll(edge, 1 if j == 0 else slots - 1, 0)
    if sums is None:
        return part, edge
    return sums[0] + part, (None if edge is None else sums[1] + edge)


def shifted_rows(sums, i, height):
    main, edge = sums
    if i == 1:
        return main
    count, out = main.shape
    width = count // height
    tile = main.reshape(width, height, out)
    moved = pltpu.roll(tile, 1 if i == 0 else height - 1, 1)
    row = lax.broadcasted_iota(jnp.int32, (height, out), 0)
    at = 0 if i == 0 else height - 1
    cells = [jnp.where(row == at, edge[c : c + 1, :], moved[c]) for c in range(width)]
    return jnp.concatenate(cells, axis=0)


def cache_conv_kernel(cache_ref, top_ref, bottom_ref, twin_ref, cross_ref, w_ref, out_ref, ext, acc):
    step = pl.program_id(0)
    width, height, channels = cache_ref.shape[1:]
    count = width * height
    odd = lax.rem(lax.axis_index("cols"), 2)

    @pl.when(step == 0)
    def _():
        for t in range(2):
            tokens = extended(
                cache_ref[t].reshape(count, channels).astype(F32),
                top_ref[t].astype(F32),
                bottom_ref[t].astype(F32),
                twin_ref[t].astype(F32),
                cross_ref[t].astype(F32),
                odd,
            )
            ext[t] = tokens.astype(BF16)

    ext_len = ext.shape[1]
    for i in range(3):

        @pl.when(step == i)
        def _():
            lo, hi = conv_rows(ext_len, top_ref.shape[1], i)
            sums = None
            for j in range(3):
                products = dot(ext[0, lo:hi, :], w_ref[0, 0, j]) + dot(ext[1, lo:hi, :], w_ref[1, 0, j])
                sums = add_taps(sums, products, i, j, height, count)
            value = shifted_rows(sums, i, height)
            if i == 0:
                acc[...] = value
            elif i == 1:
                acc[...] += value
            else:
                out_ref[...] = acc[...] + value


def cache_conv(cache, top, bottom, twin, cross, w_conv):
    _, width, height, channels = cache.shape
    out = w_conv.shape[4]
    ext_len = 2 * top.shape[1] + (width + 2) * height

    def whole(shape):
        return pl.BlockSpec(shape, lambda s: (0,) * len(shape))

    return pl.pallas_call(
        cache_conv_kernel,
        grid=(3,),
        in_specs=[
            whole(cache.shape),
            whole(top.shape),
            whole(bottom.shape),
            whole(twin.shape),
            whole(cross.shape),
            pl.BlockSpec((2, 1, 3, channels, out), lambda s: (0, s, 0, 0, 0)),
        ],
        out_specs=pl.BlockSpec((width * height, out), lambda s: (0, 0)),
        out_shape=jax.ShapeDtypeStruct((width * height, out), F32),
        scratch_shapes=[
            pltpu.VMEM((2, ext_len, channels), BF16),
            pltpu.VMEM((width * height, out), F32),
        ],
        name="cache_conv",
    )(cache, top, bottom, twin, cross, w_conv)


def query_kernel(frame_ref, top_ref, bottom_ref, twin_ref, cross_ref, gain_ref, wq_ref, wk_ref, raw_ref, keys_ref):
    width, height, channels = frame_ref.shape
    odd = lax.rem(lax.axis_index("cols"), 2)
    tokens = extended(
        frame_ref[...].reshape(width * height, channels).astype(F32),
        top_ref[...].astype(F32),
        bottom_ref[...].astype(F32),
        twin_ref[...].astype(F32),
        cross_ref[...].astype(F32),
        odd,
    )
    raw_ref[...] = tokens.astype(BF16)
    normed = rms_scaled(tokens, gain_ref[...]).astype(BF16)
    rows = (dot(normed, wq_ref[...]) * (1.0 / math.sqrt(channels))).astype(BF16)
    keys_ref[...] = dot_t(rows, wk_ref[...]).astype(BF16)


def lanes(value, width):
    return jnp.broadcast_to(value, (value.shape[0], width))


def fold_kernel(blocks, first, *refs):
    gain_ref, own_ref, twin_ref = refs[:3]
    block_refs = refs[3 : 3 + blocks]
    refs = refs[3 + blocks :]
    states, outs = ((None, None), refs) if first else (refs[:2], refs[2:])
    gain = gain_ref[...]
    keys = jnp.concatenate(
        [rms_scaled(b[...].astype(F32), gain).astype(BF16) for b in block_refs], axis=0
    )
    channels = keys.shape[1]
    for query_ref, state, out in zip((own_ref, twin_ref), states, outs):
        scores = dot_t(query_ref[...], keys)
        peak = jnp.max(scores, axis=1, keepdims=True)
        if not first:
            before = state[:, channels : channels + 1]
            peak = jnp.maximum(peak, before)
        weights = jnp.exp(scores - peak)
        total = jnp.sum(weights, axis=1, keepdims=True)
        summed = dot(weights.astype(BF16), keys)
        if not first:
            fade = jnp.exp(before - peak)
            total = total + fade * state[:, channels + 128 : channels + 129]
            summed = summed + fade * state[:, :channels]
        out[:, :channels] = summed
        out[:, channels : channels + 128] = lanes(peak, 128)
        out[:, channels + 128 :] = lanes(total, 128)


def fold(states, own, twin, gain, blocks):
    length, channels = own.shape
    shape = jax.ShapeDtypeStruct((length, channels + 256), F32)
    first = states is None
    return pl.pallas_call(
        functools.partial(fold_kernel, len(blocks), first),
        in_specs=[VM] * (3 + len(blocks) + (0 if first else 2)),
        out_specs=[VM, VM],
        out_shape=[shape, shape],
        name="fold",
    )(gain, own, twin, *blocks, *(() if first else states))


def finish_kernel(
    height, state_ref, other_ref, raw_ref, wv_ref, wo_ref, gain_ref, bias_ref, partial_ref, w_ref,
    hidden_ref, mixed_ref, w_buf, sem,
):
    fetch = pltpu.make_async_copy(w_ref.at[2], w_buf, sem)
    fetch.start()
    length, channels = raw_ref.shape
    count, out = partial_ref.shape
    slots = edge_slots(count // height)
    row = lax.axis_index("rows")
    col = lax.axis_index("cols")
    has_top, has_bottom = row > 0, row < lax.axis_size("rows") - 1
    has_left, has_right = col > 0, col < lax.axis_size("cols") - 1

    peak_a, peak_b = state_ref[:, channels : channels + 1], other_ref[:, channels : channels + 1]
    peak = jnp.maximum(peak_a, peak_b)
    fade_a, fade_b = jnp.exp(peak_a - peak), jnp.exp(peak_b - peak)
    total = fade_a * state_ref[:, channels + 128 : channels + 129]
    total = total + fade_b * other_ref[:, channels + 128 : channels + 129]
    summed = fade_a * state_ref[:, :channels] + fade_b * other_ref[:, :channels]
    pooled = (summed / total).astype(BF16)
    attended = dot(pooled, wv_ref[...]).astype(BF16)
    hidden = (raw_ref[...].astype(F32) + dot(attended, wo_ref[...])).astype(BF16)
    wide = hidden.astype(F32)
    value = rms_scaled(wide, gain_ref[...])
    value = value / (1.0 + jnp.exp(-value))
    slot = lax.broadcasted_iota(jnp.int32, (length, 1), 0)
    main_end = length - slots
    width = count // height
    in_top, in_bottom = slot < slots, slot >= main_end
    in_left = (slot >= slots) & (slot < slots + height)
    in_right = (slot >= main_end - height) & (slot < main_end)
    in_left = in_left | (slot == slots - 1) | (slot == length - 1)
    in_right = in_right | (slot == width) | (slot == main_end + width)
    outside = (in_top & jnp.logical_not(has_top)) | (in_bottom & jnp.logical_not(has_bottom))
    outside = outside | (in_left & jnp.logical_not(has_left)) | (in_right & jnp.logical_not(has_right))
    ext = jnp.where(outside, 0.0, value).astype(BF16)

    own = hidden[slots + height : slots + height + count]
    hidden_ref[...] = own
    result = partial_ref[...] + own[:, :out].astype(F32) + bias_ref[...]
    fetch.wait()
    for i in range(3):
        lo, hi = conv_rows(length, slots, i)
        sums = None
        for j in range(3):
            sums = add_taps(sums, dot(ext[lo:hi], w_buf[i, j]), i, j, height, count)
        result = result + shifted_rows(sums, i, height)
    mixed_ref[...] = result.astype(BF16)


def finish(height, state, other, raw, w_value, w_out, gain, bias, partial, w_conv):
    count, out = partial.shape
    channels = raw.shape[1]
    return pl.pallas_call(
        functools.partial(finish_kernel, height),
        in_specs=[VM] * 8 + [pl.BlockSpec(memory_space=pl.ANY)],
        out_specs=[VM, VM],
        out_shape=[
            jax.ShapeDtypeStruct((count, channels), BF16),
            jax.ShapeDtypeStruct((count, out), BF16),
        ],
        scratch_shapes=[pltpu.VMEM(w_conv.shape[1:], BF16), pltpu.SemaphoreType.DMA],
        name="finish",
    )(state, other, raw, w_value, w_out, gain, bias, partial, w_conv)


def body(
    frame_in, norm_gain, w_query, w_key, w_value, w_out, conv_gain, conv_cache, w_conv, conv_bias
):
    height, width, channels = frame_in.shape
    out_channels = w_conv.shape[4]
    count = height * width
    chips, ring, twin_pairs, down, up, cross_pairs = permutations(
        lax.axis_size("rows"), lax.axis_size("cols")
    )
    frame = jnp.transpose(frame_in, (1, 0, 2))
    cache = jnp.transpose(conv_cache, (0, 2, 1, 3))
    own = frame.reshape(count, channels)
    gain = norm_gain.reshape(1, channels)

    chain_a = own
    chain_b = lax.ppermute(own, AXES, twin_pairs)
    blocks = [[own]]
    hops = chips // 2
    for hop in range(hops):
        chain_a = lax.ppermute(chain_a, AXES, ring)
        arrived = [chain_a]
        if hop < hops - 1 or chips % 2:
            chain_b = lax.ppermute(chain_b, AXES, ring)
            arrived.append(chain_b)
        blocks.append(arrived)

    edge = jax.ShapeDtypeStruct((3, edge_slots(width), channels), BF16)
    first, last = pl.pallas_call(
        pack_rows_kernel, in_specs=[VM, VM], out_specs=[VM, VM], out_shape=[edge, edge], name="pack_rows"
    )(frame, cache)
    top = lax.ppermute(last, AXES, down)
    bottom = lax.ppermute(first, AXES, up)
    side = jax.ShapeDtypeStruct((3, side_slots(height), channels), BF16)
    to_twin, to_cross = pl.pallas_call(
        pack_cols_kernel, in_specs=[VM] * 4, out_specs=[VM, VM], out_shape=[side, side], name="pack_cols"
    )(frame, cache, top, bottom)
    twin = lax.ppermute(to_twin, AXES, twin_pairs)
    cross = lax.ppermute(to_cross, AXES, cross_pairs)

    length = 2 * edge_slots(width) + (width + 2) * height
    ext_shape = jax.ShapeDtypeStruct((length, channels), BF16)
    raw, queries = pl.pallas_call(
        query_kernel, in_specs=[VM] * 8, out_specs=[VM, VM], out_shape=[ext_shape, ext_shape], name="query"
    )(frame, top[2], bottom[2], twin[2], cross[2], gain, w_query, w_key)
    twin_queries = lax.ppermute(queries, AXES, twin_pairs)
    partial = cache_conv(cache, top, bottom, twin, cross, w_conv)

    groups, waiting = [], []
    for hop, arrived in enumerate(blocks):
        waiting = waiting + arrived
        if hop >= len(blocks) - 2 or len(waiting) >= 5:
            groups.append(waiting)
            waiting = []
    states = None
    for group in groups:
        states = fold(states, queries, twin_queries, gain, group)
    other = lax.ppermute(states[1], AXES, twin_pairs)
    hidden, mixed = finish(
        height, states[0], other, raw, w_value, w_out, conv_gain.reshape(1, channels),
        conv_bias.reshape(1, out_channels), partial, w_conv,
    )
    hidden = jnp.transpose(hidden.reshape(width, height, channels), (1, 0, 2))
    mixed = jnp.transpose(mixed.reshape(width, height, out_channels), (1, 0, 2))
    return (hidden, mixed)


def solution(mesh):
    in_specs = (
        P(("video", "rows"), "cols", None),
        P(),
        P(),
        P(),
        P(),
        P(),
        P(),
        P(None, ("video", "rows"), "cols", None),
        P(),
        P(),
    )
    out_specs = (P(("video", "rows"), "cols", None), P(("video", "rows"), "cols", None))
    return jax.shard_map(body, mesh=mesh, in_specs=in_specs, out_specs=out_specs, check_vma=False)
```

```python
import functools
import math

import jax
import jax.numpy as jnp
from jax import lax
from jax.experimental import pallas as pl
from jax.experimental.pallas import tpu as pltpu
from jax.sharding import PartitionSpec as P


EPS = 1e-06
AXES = ("rows", "cols")
F32 = jnp.float32
BF16 = jnp.bfloat16
VM = pl.BlockSpec(memory_space=pltpu.VMEM)


def near(value):
    return pltpu.with_memory_space_constraint(value, pltpu.VMEM)


def call(kernel, outs, args, limit=16 << 20, far_args=(), far=False, scratch=()):
    return pl.pallas_call(
        kernel,
        in_specs=[VM] * len(args) + [pl.BlockSpec(memory_space=pltpu.HBM)] * len(far_args),
        out_specs=[VM] * len(outs),
        out_shape=[
            jax.ShapeDtypeStruct(shape, dtype) if far else pltpu.VMEM(shape, dtype)
            for shape, dtype in outs
        ],
        scratch_shapes=scratch,
        compiler_params=pltpu.CompilerParams(vmem_limit_bytes=limit),
    )(*[near(a) for a in args], *[pltpu.with_memory_space_constraint(a, pltpu.HBM) for a in far_args])


def buffers(*arrays):
    return [pltpu.VMEM(a.shape, a.dtype) for a in arrays] + [pltpu.SemaphoreType.DMA((len(arrays),))]


def chip_cycle(height, width):
    if width == 1 or height == 1:
        return [(z, x) for z in range(height) for x in range(width)]
    order = []
    for x in range(width):
        inner = range(1, height) if x % 2 == 0 else range(height - 1, 0, -1)
        order += [(z, x) for z in inner]
    return order + [(0, x) for x in range(width - 1, -1, -1)]


def permutations(rows, cols):
    def at(z, x, core):
        return z * cols + 2 * x + core

    walk = chip_cycle(rows, cols // 2)
    ring = []
    for k, here in enumerate(walk):
        there = walk[(k + 1) % len(walk)]
        ring += [(at(*here, 0), at(*there, 0)), (at(*there, 1), at(*here, 1))]
    twin = [(i, i ^ 1) for i in range(rows * cols)]
    down = [(i, i + cols) for i in range((rows - 1) * cols)]
    up = [(j, i) for i, j in down]
    cross = []
    for r in range(rows):
        for c in range(1, cols - 1, 2):
            i = r * cols + c
            cross += [(i, i + 1), (i + 1, i)]
    return len(walk), ring, twin, down, up, cross


def edge_slots(width):
    return -(-(width + 2) // 16) * 16


def edge_rows(width):
    return -(-width // 8) * 8


def side_slots(height):
    return height + 8


def rms_scaled(values, gain):
    mean_sq = jnp.mean(values * values, axis=-1, keepdims=True)
    return values * lax.rsqrt(mean_sq + EPS) * gain


def dot(a, b):
    return jnp.dot(a, b, preferred_element_type=F32)


def dot_t(a, b):
    return lax.dot_general(a, b, (((1,), (1,)), ((), ())), preferred_element_type=F32)


def pack_rows_kernel(frame_hbm, cache_hbm, gain_hbm, frame_ref, cache_ref, gain_ref, first_ref, last_ref, sems):
    copies = [
        pltpu.make_async_copy(frame_hbm, frame_ref, sems.at[0]),
        pltpu.make_async_copy(cache_hbm, cache_ref, sems.at[1]),
        pltpu.make_async_copy(gain_hbm, gain_ref, sems.at[2]),
    ]
    for copy in copies:
        copy.start()
    for copy in copies:
        copy.wait()
    width, height, channels = frame_ref.shape
    fill = jnp.zeros((edge_rows(width) - width, channels), F32)
    for t in range(3):
        tile = (frame_ref[...] if t == 2 else cache_ref[t]).astype(F32)
        for r, out in ((0, first_ref), (height - 1, last_ref)):
            row = jnp.concatenate([tile[c, r : r + 1, :] for c in range(width)] + [fill], axis=0)
            out[t] = row.astype(BF16)


def pack_cols_kernel(frame_ref, cache_ref, top_ref, bottom_ref, twin_ref, cross_ref):
    width, height, channels = frame_ref.shape
    odd = lax.rem(lax.axis_index("cols"), 2)
    fill = jnp.zeros((side_slots(height) - height - 2, channels), F32)
    for t in range(3):
        sides = []
        for c in (0, width - 1):
            own = (frame_ref[c] if t == 2 else cache_ref[t, c]).astype(F32)
            top = top_ref[t].astype(F32)[c : c + 1, :]
            bottom = bottom_ref[t].astype(F32)[c : c + 1, :]
            sides.append(jnp.concatenate([own, top, bottom, fill], axis=0))
        left, right = sides
        twin_ref[t] = jnp.where(odd == 1, left, right).astype(BF16)
        cross_ref[t] = jnp.where(odd == 1, right, left).astype(BF16)


def extended(own, top, bottom, twin, cross, odd):
    height = twin.shape[0] - side_slots(0)
    left = jnp.where(odd == 1, twin, cross)
    right = jnp.where(odd == 1, cross, twin)
    width = own.shape[0] // height
    slots = edge_slots(width)
    slot = lax.broadcasted_iota(jnp.int32, (slots, own.shape[1]), 0)
    fill = jnp.zeros((slots - top.shape[0], own.shape[1]), F32)

    def edge(row, k):
        row = jnp.concatenate([row, fill], axis=0)
        row = jnp.where(slot == width, right[k : k + 1, :], row)
        return jnp.where(slot == slots - 1, left[k : k + 1, :], row)

    return jnp.concatenate(
        [edge(top, height), left[:height], own, right[:height], edge(bottom, height + 1)], axis=0
    )


def conv_rows(ext_len, slots, i):
    return (0 if i == 0 else slots), (ext_len if i == 2 else ext_len - slots)


def add_taps(sums, products, i, j, height, count):
    slots = edge_slots(count // height)
    main = products[slots:] if i == 0 else products
    part = main[j * height : j * height + count]
    edge = None
    if i == 0:
        edge = products[:slots]
    if i == 2:
        edge = products[products.shape[0] - slots :]
    if edge is not None and j != 1:
        edge = pltpu.roll(edge, 1 if j == 0 else slots - 1, 0)
    if sums is None:
        return part, edge
    return sums[0] + part, (None if edge is None else sums[1] + edge)


def shifted_rows(sums, i, height):
    main, edge = sums
    if i == 1:
        return main
    count, out = main.shape
    width = count // height
    tile = main.reshape(width, height, out)
    moved = pltpu.roll(tile, 1 if i == 0 else height - 1, 1)
    row = lax.broadcasted_iota(jnp.int32, (height, out), 0)
    at = 0 if i == 0 else height - 1
    cells = [jnp.where(row == at, edge[c : c + 1, :], moved[c]) for c in range(width)]
    return jnp.concatenate(cells, axis=0)


def cache_conv_kernel(
    cache_ref, top_ref, bottom_ref, twin_ref, cross_ref, w_hbm, out_ref, w_ref, sems
):
    copies = [
        pltpu.make_async_copy(w_hbm.at[pl.ds(0, 2), i], w_ref.at[i], sems.at[i]) for i in range(3)
    ]
    for copy in copies:
        copy.start()
    width, height, channels = cache_ref.shape[1:]
    count = width * height
    odd = lax.rem(lax.axis_index("cols"), 2)
    exts = [
        extended(
            cache_ref[t].reshape(count, channels).astype(F32),
            top_ref[t].astype(F32),
            bottom_ref[t].astype(F32),
            twin_ref[t].astype(F32),
            cross_ref[t].astype(F32),
            odd,
        ).astype(BF16)
        for t in range(2)
    ]
    result = None
    for i in range(3):
        lo, hi = conv_rows(exts[0].shape[0], edge_slots(width), i)
        sums = None
        copies[i].wait()
        for j in range(3):
            products = dot(exts[0][lo:hi], w_ref[i, 0, j]) + dot(exts[1][lo:hi], w_ref[i, 1, j])
            sums = add_taps(sums, products, i, j, height, count)
        value = shifted_rows(sums, i, height)
        result = value if result is None else result + value
    out_ref[...] = result


def query_kernel(
    frame_ref, top_ref, bottom_ref, twin_ref, cross_ref, gain_ref, wq_hbm, wk_hbm, raw_ref, keys_ref,
    wq_ref, wk_ref, sems,
):
    copies = [
        pltpu.make_async_copy(wq_hbm, wq_ref, sems.at[0]),
        pltpu.make_async_copy(wk_hbm, wk_ref, sems.at[1]),
    ]
    for copy in copies:
        copy.start()
    width, height, channels = frame_ref.shape
    odd = lax.rem(lax.axis_index("cols"), 2)
    tokens = extended(
        frame_ref[...].reshape(width * height, channels).astype(F32),
        top_ref[2].astype(F32),
        bottom_ref[2].astype(F32),
        twin_ref[2].astype(F32),
        cross_ref[2].astype(F32),
        odd,
    )
    raw_ref[...] = tokens.astype(BF16)
    normed = rms_scaled(tokens, gain_ref[...]).astype(BF16)
    copies[0].wait()
    rows = (dot(normed, wq_ref[...]) * (1.0 / math.sqrt(channels))).astype(BF16)
    copies[1].wait()
    keys_ref[...] = dot_t(rows, wk_ref[...]).astype(BF16)


def lanes(value, width):
    return jnp.broadcast_to(value, (value.shape[0], width))


def key_rows(refs, gain):
    parts = [
        rms_scaled(ref[...].reshape(-1, gain.shape[1]).astype(F32), gain).astype(BF16) for ref in refs
    ]
    return parts[0] if len(parts) == 1 else jnp.concatenate(parts, axis=0)


def fold_kernel(blocks, first, gain_ref, own_ref, twin_ref, *refs):
    keys = key_rows(refs[:blocks], gain_ref[...])
    states, outs = ((None, None), refs[blocks:]) if first else (refs[blocks:-2], refs[-2:])
    channels = keys.shape[1]
    length = own_ref.shape[0]
    all_scores = dot_t(jnp.concatenate([own_ref[...], twin_ref[...]], axis=0), keys)
    peaks, totals, weights = [], [], []
    for k, state in enumerate(states):
        scores = all_scores[k * length : (k + 1) * length]
        peak = jnp.max(scores, axis=1, keepdims=True)
        if not first:
            peak = jnp.maximum(peak, state[:, channels : channels + 1])
        part = jnp.exp(scores - peak)
        peaks.append(peak)
        totals.append(jnp.sum(part, axis=1, keepdims=True))
        weights.append(part.astype(BF16))
    all_summed = dot(jnp.concatenate(weights, axis=0), keys)
    for k, (state, out) in enumerate(zip(states, outs)):
        summed, total, peak = all_summed[k * length : (k + 1) * length], totals[k], peaks[k]
        if not first:
            fade = jnp.exp(state[:, channels : channels + 1] - peak)
            total = total + fade * state[:, channels + 128 : channels + 129]
            summed = summed + fade * state[:, :channels]
        out[:, :channels] = summed
        out[:, channels : channels + 128] = lanes(peak, 128)
        out[:, channels + 128 :] = lanes(total, 128)


def fold(states, own, twin, gain, blocks):
    length, channels = own.shape
    shape = ((length, channels + 256), F32)
    first = states is None
    args = (gain, own, twin, *blocks, *(() if first else states))
    return call(functools.partial(fold_kernel, len(blocks), first), [shape, shape], args, 24 << 20)


def finish_kernel(
    height, state_ref, other_ref, query_ref, last_ref, swapped_ref, key_gain_ref, raw_ref, partial_ref,
    wv_hbm, wo_hbm, gain_hbm, bias_hbm, w_hbm, hidden_ref, mixed_ref,
    wv_ref, wo_ref, gain_ref, bias_ref, w_ref, sems,
):
    copies = [
        pltpu.make_async_copy(wv_hbm, wv_ref, sems.at[0]),
        pltpu.make_async_copy(wo_hbm, wo_ref, sems.at[1]),
        pltpu.make_async_copy(gain_hbm, gain_ref, sems.at[2]),
        pltpu.make_async_copy(bias_hbm, bias_ref, sems.at[3]),
        pltpu.make_async_copy(w_hbm.at[2], w_ref, sems.at[4]),
    ]
    for copy in copies:
        copy.start()
    length, channels = raw_ref.shape
    count, out = partial_ref.shape
    slots = edge_slots(count // height)
    row = lax.axis_index("rows")
    col = lax.axis_index("cols")
    has_top, has_bottom = row > 0, row < lax.axis_size("rows") - 1
    has_left, has_right = col > 0, col < lax.axis_size("cols") - 1

    keys = key_rows((last_ref, swapped_ref), key_gain_ref[...])
    scores = dot_t(query_ref[...], keys)
    peak_a, peak_b = state_ref[:, channels : channels + 1], other_ref[:, channels : channels + 1]
    peak = jnp.maximum(jnp.maximum(peak_a, peak_b), jnp.max(scores, axis=1, keepdims=True))
    fade_a, fade_b = jnp.exp(peak_a - peak), jnp.exp(peak_b - peak)
    weights = jnp.exp(scores - peak)
    total = jnp.sum(weights, axis=1, keepdims=True)
    total = total + fade_a * state_ref[:, channels + 128 : channels + 129]
    total = total + fade_b * other_ref[:, channels + 128 : channels + 129]
    summed = dot(weights.astype(BF16), keys)
    summed = summed + fade_a * state_ref[:, :channels] + fade_b * other_ref[:, :channels]
    pooled = (summed / total).astype(BF16)
    for copy in copies:
        copy.wait()
    attended = dot(pooled, wv_ref[...]).astype(BF16)
    hidden = (raw_ref[...].astype(F32) + dot(attended, wo_ref[...])).astype(BF16)
    wide = hidden.astype(F32)
    value = rms_scaled(wide, gain_ref[...])
    value = value / (1.0 + jnp.exp(-value))
    slot = lax.broadcasted_iota(jnp.int32, (length, 1), 0)
    main_end = length - slots
    width = count // height
    in_top, in_bottom = slot < slots, slot >= main_end
    in_left = (slot >= slots) & (slot < slots + height)
    in_right = (slot >= main_end - height) & (slot < main_end)
    in_left = in_left | (slot == slots - 1) | (slot == length - 1)
    in_right = in_right | (slot == width) | (slot == main_end + width)
    outside = (in_top & jnp.logical_not(has_top)) | (in_bottom & jnp.logical_not(has_bottom))
    outside = outside | (in_left & jnp.logical_not(has_left)) | (in_right & jnp.logical_not(has_right))
    ext = jnp.where(outside, 0.0, value).astype(BF16)

    own = hidden[slots + height : slots + height + count]
    hidden_ref[...] = own
    result = partial_ref[...] + own[:, :out].astype(F32) + bias_ref[...]
    for i in range(3):
        lo, hi = conv_rows(length, slots, i)
        sums = None
        for j in range(3):
            sums = add_taps(sums, dot(ext[lo:hi], w_ref[i, j]), i, j, height, count)
        result = result + shifted_rows(sums, i, height)
    mixed_ref[...] = result.astype(BF16)


def join_kernel(a_ref, b_ref, out_ref):
    count = b_ref.shape[0]
    out_ref[:count] = a_ref[...].reshape(b_ref.shape)
    out_ref[count:] = b_ref[...]


def moved(value, pairs):
    return lax.ppermute(value, AXES, pairs)


def block(
    frame_in, norm_gain, w_query, w_key, w_value, w_out, conv_gain, conv_cache, w_conv, conv_bias
):
    height, width, channels = frame_in.shape
    out_channels = w_conv.shape[4]
    count = height * width
    chips, ring, twin_pairs, down, up, cross_pairs = permutations(
        lax.axis_size("rows"), lax.axis_size("cols")
    )
    frame_far = jnp.transpose(frame_in, (1, 0, 2))
    cache_far = jnp.transpose(conv_cache, (0, 2, 1, 3))
    gain_far = norm_gain.reshape(1, channels)

    edge = ((3, edge_rows(width), channels), BF16)
    frame, cache, gain, first_rows, last_rows = call(
        pack_rows_kernel,
        [(frame_far.shape, BF16), (cache_far.shape, BF16), (gain_far.shape, F32), edge, edge],
        (),
        far_args=(frame_far, cache_far, gain_far),
        scratch=[pltpu.SemaphoreType.DMA((3,))],
    )

    partner = moved(frame_far.reshape(count, channels), twin_pairs)
    (chain,) = call(join_kernel, [((2 * count, channels), BF16)], (frame, partner))
    blocks = [frame]
    hops = (chips - 1) // 2
    for _ in range(hops):
        chain = moved(chain, ring)
        blocks.append(chain)
    last = moved(chain[:count], ring)
    swapped = moved(last, twin_pairs)

    top = moved(last_rows, down)
    bottom = moved(first_rows, up)
    side = ((3, side_slots(height), channels), BF16)
    to_twin, to_cross = call(pack_cols_kernel, [side, side], (frame, cache, top, bottom))
    twin = moved(to_twin, twin_pairs)
    cross = moved(to_cross, cross_pairs)

    ext = ((2 * edge_slots(width) + (width + 2) * height, channels), BF16)
    raw, queries = call(
        query_kernel, [ext, ext], (frame, top, bottom, twin, cross, gain),
        far_args=(w_query, w_key), scratch=buffers(w_query, w_key),
    )
    twin_queries = moved(queries, twin_pairs)
    (partial,) = call(
        cache_conv_kernel, [((count, out_channels), F32)], (cache, top, bottom, twin, cross),
        far_args=(w_conv,),
        scratch=[
            pltpu.VMEM((3, 2) + w_conv.shape[2:], BF16),
            pltpu.SemaphoreType.DMA((3,)),
        ],
    )
    states = None
    for k in range(0, len(blocks), 4):
        states = fold(states, queries, twin_queries, gain, blocks[k : k + 4])
    other = moved(states[1], twin_pairs)
    far_args = (
        w_value, w_out, conv_gain.reshape(1, channels), conv_bias.reshape(1, out_channels), w_conv
    )
    hidden, mixed = call(
        functools.partial(finish_kernel, height),
        [((count, channels), BF16), ((count, out_channels), BF16)],
        (states[0], other, queries, last, swapped, gain, raw, partial),
        24 << 20,
        far_args,
        True,
        buffers(*far_args[:4], jax.ShapeDtypeStruct(w_conv.shape[1:], BF16)),
    )
    hidden = jnp.transpose(hidden.reshape(width, height, channels), (1, 0, 2))
    mixed = jnp.transpose(mixed.reshape(width, height, out_channels), (1, 0, 2))
    return (hidden, mixed)


def solution(mesh):
    in_specs = (
        P(("video", "rows"), "cols", None),
        P(),
        P(),
        P(),
        P(),
        P(),
        P(),
        P(None, ("video", "rows"), "cols", None),
        P(),
        P(),
    )
    out_specs = (P(("video", "rows"), "cols", None), P(("video", "rows"), "cols", None))
    return jax.shard_map(block, mesh=mesh, in_specs=in_specs, out_specs=out_specs, check_vma=False)
```

```python
import functools
import math

import jax
import jax.numpy as jnp
from jax import lax
from jax.experimental import pallas as pl
from jax.experimental.pallas import tpu as pltpu
from jax.sharding import PartitionSpec as P


EPS = 1e-06
AXES = ("rows", "cols")
F32 = jnp.float32
BF16 = jnp.bfloat16
VM = pl.BlockSpec(memory_space=pltpu.VMEM)


def near(value):
    return pltpu.with_memory_space_constraint(value, pltpu.VMEM)


def call(kernel, outs, args, limit=16 << 20, far_args=(), far=False, scratch=()):
    return pl.pallas_call(
        kernel,
        in_specs=[VM] * len(args) + [pl.BlockSpec(memory_space=pltpu.HBM)] * len(far_args),
        out_specs=[VM] * len(outs),
        out_shape=[
            jax.ShapeDtypeStruct(shape, dtype) if far else pltpu.VMEM(shape, dtype)
            for shape, dtype in outs
        ],
        scratch_shapes=scratch,
        compiler_params=pltpu.CompilerParams(vmem_limit_bytes=limit),
    )(*[near(a) for a in args], *[pltpu.with_memory_space_constraint(a, pltpu.HBM) for a in far_args])


def chip_cycle(height, width):
    if width == 1 or height == 1:
        return [(z, x) for z in range(height) for x in range(width)]
    order = []
    for x in range(width):
        inner = range(1, height) if x % 2 == 0 else range(height - 1, 0, -1)
        order += [(z, x) for z in inner]
    return order + [(0, x) for x in range(width - 1, -1, -1)]


def permutations(rows, cols):
    def at(z, x, core):
        return z * cols + 2 * x + core

    walk = chip_cycle(rows, cols // 2)
    ring = []
    for k, here in enumerate(walk):
        there = walk[(k + 1) % len(walk)]
        ring += [(at(*here, 0), at(*there, 0)), (at(*there, 1), at(*here, 1))]
    twin = [(i, i ^ 1) for i in range(rows * cols)]
    down = [(i, i + cols) for i in range((rows - 1) * cols)]
    up = [(j, i) for i, j in down]
    cross = []
    for r in range(rows):
        for c in range(1, cols - 1, 2):
            i = r * cols + c
            cross += [(i, i + 1), (i + 1, i)]
    return len(walk), ring, twin, down, up, cross


def edge_slots(width):
    return -(-(width + 2) // 16) * 16


def edge_rows(width):
    return -(-width // 8) * 8


def side_slots(height):
    return height + 8


def rms_scaled(values, gain):
    mean_sq = jnp.mean(values * values, axis=-1, keepdims=True)
    return values * lax.rsqrt(mean_sq + EPS) * gain


def dot(a, b):
    return jnp.dot(a, b, preferred_element_type=F32)


def dot_t(a, b):
    return lax.dot_general(a, b, (((1,), (1,)), ((), ())), preferred_element_type=F32)


def row_edge(tile, r):
    width, _, channels = tile.shape
    fill = jnp.zeros((edge_rows(width) - width, channels), F32)
    return jnp.concatenate([tile[c, r : r + 1, :] for c in range(width)] + [fill], axis=0)


def load_tiles(frame_hbm, cache_hbm, gain_hbm, frame_ref, cache_ref, gain_ref, sems):
    copies = [
        pltpu.make_async_copy(frame_hbm, frame_ref, sems.at[0]),
        pltpu.make_async_copy(cache_hbm, cache_ref, sems.at[1]),
        pltpu.make_async_copy(gain_hbm, gain_ref, sems.at[2]),
    ]
    for copy in copies:
        copy.start()
    for copy in copies:
        copy.wait()


def pack_rows_kernel(frame_hbm, cache_hbm, gain_hbm, frame_ref, cache_ref, gain_ref, first_ref, last_ref, sems):
    load_tiles(frame_hbm, cache_hbm, gain_hbm, frame_ref, cache_ref, gain_ref, sems)
    height = frame_ref.shape[1]
    for t in range(3):
        tile = (frame_ref[...] if t == 2 else cache_ref[t]).astype(F32)
        first_ref[t] = row_edge(tile, 0).astype(BF16)
        last_ref[t] = row_edge(tile, height - 1).astype(BF16)


def faces_up():
    col = lax.axis_index("cols")
    return lax.rem(lax.rem(col, 2) + lax.div(col, 2), 2)


def pack_swap_kernel(frame_hbm, cache_hbm, gain_hbm, frame_ref, cache_ref, gain_ref, edge_ref, swap_ref, sems):
    load_tiles(frame_hbm, cache_hbm, gain_hbm, frame_ref, cache_ref, gain_ref, sems)
    width, height, channels = frame_ref.shape
    count, rows = width * height, edge_rows(width)
    up = faces_up()
    odd = lax.rem(lax.axis_index("cols"), 2)
    swap_ref[:count] = frame_ref[...].reshape(count, channels)
    for t in range(2):
        tile = cache_ref[t].astype(F32)
        first, last = row_edge(tile, 0), row_edge(tile, height - 1)
        edge_ref[t * rows : (t + 1) * rows] = jnp.where(up == 1, first, last).astype(BF16)
        at = count + t * rows
        swap_ref[at : at + rows] = jnp.where(up == 1, last, first).astype(BF16)
        at = count + 2 * rows + t * height
        swap_ref[at : at + height] = jnp.where(odd == 1, tile[0], tile[width - 1]).astype(BF16)


def join_edges_kernel(frame_ref, edge_ref, partner_ref, out_ref):
    width, height, channels = frame_ref.shape
    count, rows = width * height, edge_ref.shape[0]
    out_ref[:count] = frame_ref[...].reshape(count, channels)
    out_ref[count : 2 * count] = partner_ref[:count]
    out_ref[2 * count : 2 * count + rows] = edge_ref[...]
    out_ref[2 * count + rows :] = partner_ref[count : count + rows]


def split_kernel(height, arrived_ref, chain_ref, edges_ref):
    count = chain_ref.shape[0] // 2
    width = count // height
    rows = edge_rows(width)
    up = faces_up()
    chain_ref[...] = arrived_ref[: 2 * count]
    for k in range(2):
        to = k * 3 * rows
        at = 2 * count + k * 2 * rows
        edges_ref[to : to + 2 * rows] = arrived_ref[at : at + 2 * rows]
        tile = arrived_ref[k * count : (k + 1) * count].astype(F32).reshape(width, height, -1)
        edge = jnp.where(up == 1, row_edge(tile, 0), row_edge(tile, height - 1))
        edges_ref[to + 2 * rows : to + 3 * rows] = edge.astype(BF16)


def sort_edges_kernel(
    frame_ref, cache_ref, partner_ref, mine_ref, theirs_ref, top_ref, bottom_ref, twin_ref, cross_ref
):
    width, height, channels = frame_ref.shape
    count, rows = width * height, top_ref.shape[1]
    up = faces_up()
    odd = lax.rem(lax.axis_index("cols"), 2)
    row = lax.axis_index("rows")
    has_top, has_bottom = row > 0, row < lax.axis_size("rows") - 1
    fill = jnp.zeros((side_slots(height) - height - 2, channels), F32)
    for t in range(3):
        pair = []
        for k in range(2):
            mine = mine_ref[(3 * k + t) * rows : (3 * k + t + 1) * rows].astype(F32)
            theirs = theirs_ref[(3 - 3 * k + t) * rows : (4 - 3 * k + t) * rows].astype(F32)
            top = jnp.where(has_top, jnp.where(up == 1, theirs, mine), 0.0)
            bottom = jnp.where(has_bottom, jnp.where(up == 1, mine, theirs), 0.0)
            pair.append((top, bottom))
        (top, bottom), (twin_top, twin_bottom) = pair
        top_ref[t] = top.astype(BF16)
        bottom_ref[t] = bottom.astype(BF16)

        def facing(first, value, axis_rows):
            a, b = value[axis_rows(0)], value[axis_rows(width - 1)]
            return jnp.where(first, a, b)

        if t == 2:
            block = partner_ref[:count].astype(F32)
            column = facing(odd == 0, block, lambda c: slice(c * height, (c + 1) * height))
        else:
            at = count + 2 * rows + t * height
            column = partner_ref[at : at + height].astype(F32)
        corners = [facing(odd == 0, v, lambda c: slice(c, c + 1)) for v in (twin_top, twin_bottom)]
        twin_ref[t] = jnp.concatenate([column, *corners, fill], axis=0).astype(BF16)
        tile = (frame_ref[...] if t == 2 else cache_ref[t]).astype(F32)
        column = jnp.where(odd == 0, tile[0], tile[width - 1])
        corners = [facing(odd == 0, v, lambda c: slice(c, c + 1)) for v in (top, bottom)]
        cross_ref[t] = jnp.concatenate([column, *corners, fill], axis=0).astype(BF16)


def pack_cols_kernel(frame_ref, cache_ref, top_ref, bottom_ref, twin_ref, cross_ref):
    width, height, channels = frame_ref.shape
    odd = lax.rem(lax.axis_index("cols"), 2)
    fill = jnp.zeros((side_slots(height) - height - 2, channels), F32)
    for t in range(3):
        sides = []
        for c in (0, width - 1):
            own = (frame_ref[c] if t == 2 else cache_ref[t, c]).astype(F32)
            top = top_ref[t].astype(F32)[c : c + 1, :]
            bottom = bottom_ref[t].astype(F32)[c : c + 1, :]
            sides.append(jnp.concatenate([own, top, bottom, fill], axis=0))
        left, right = sides
        twin_ref[t] = jnp.where(odd == 1, left, right).astype(BF16)
        cross_ref[t] = jnp.where(odd == 1, right, left).astype(BF16)


def extended(own, top, bottom, twin, cross, odd):
    height = twin.shape[0] - side_slots(0)
    left = jnp.where(odd == 1, twin, cross)
    right = jnp.where(odd == 1, cross, twin)
    width = own.shape[0] // height
    slots = edge_slots(width)
    slot = lax.broadcasted_iota(jnp.int32, (slots, own.shape[1]), 0)
    fill = jnp.zeros((slots - top.shape[0], own.shape[1]), F32)

    def edge(row, k):
        row = jnp.concatenate([row, fill], axis=0)
        row = jnp.where(slot == width, right[k : k + 1, :], row)
        return jnp.where(slot == slots - 1, left[k : k + 1, :], row)

    return jnp.concatenate(
        [edge(top, height), left[:height], own, right[:height], edge(bottom, height + 1)], axis=0
    )


def conv_rows(ext_len, slots, i):
    return (0 if i == 0 else slots), (ext_len if i == 2 else ext_len - slots)


def add_taps(sums, products, i, j, height, count):
    slots = edge_slots(count // height)
    main = products[slots:] if i == 0 else products
    part = main[j * height : j * height + count]
    edge = None
    if i == 0:
        edge = products[:slots]
    if i == 2:
        edge = products[products.shape[0] - slots :]
    if edge is not None and j != 1:
        edge = pltpu.roll(edge, 1 if j == 0 else slots - 1, 0)
    if sums is None:
        return part, edge
    return sums[0] + part, (None if edge is None else sums[1] + edge)


def shifted_rows(sums, i, height):
    main, edge = sums
    if i == 1:
        return main
    count, out = main.shape
    width = count // height
    tile = main.reshape(width, height, out)
    moved = pltpu.roll(tile, 1 if i == 0 else height - 1, 1)
    row = lax.broadcasted_iota(jnp.int32, (height, out), 0)
    at = 0 if i == 0 else height - 1
    cells = [jnp.where(row == at, edge[c : c + 1, :], moved[c]) for c in range(width)]
    return jnp.concatenate(cells, axis=0)


def cache_conv_kernel(cache_ref, top_ref, bottom_ref, twin_ref, cross_ref, w_ref, out_ref):
    width, height, channels = cache_ref.shape[1:]
    count = width * height
    odd = lax.rem(lax.axis_index("cols"), 2)
    exts = [
        extended(
            cache_ref[t].reshape(count, channels).astype(F32),
            top_ref[t].astype(F32),
            bottom_ref[t].astype(F32),
            twin_ref[t].astype(F32),
            cross_ref[t].astype(F32),
            odd,
        ).astype(BF16)
        for t in range(2)
    ]
    result = None
    for i in range(3):
        lo, hi = conv_rows(exts[0].shape[0], edge_slots(width), i)
        sums = None
        for j in range(3):
            products = dot(exts[0][lo:hi], w_ref[0, i, j]) + dot(exts[1][lo:hi], w_ref[1, i, j])
            sums = add_taps(sums, products, i, j, height, count)
        value = shifted_rows(sums, i, height)
        result = value if result is None else result + value
    out_ref[...] = result


def query_kernel(
    frame_ref, top_ref, bottom_ref, twin_ref, cross_ref, gain_ref, wq_ref, wk_ref, raw_ref, keys_ref
):
    width, height, channels = frame_ref.shape
    odd = lax.rem(lax.axis_index("cols"), 2)
    tokens = extended(
        frame_ref[...].reshape(width * height, channels).astype(F32),
        top_ref[2].astype(F32),
        bottom_ref[2].astype(F32),
        twin_ref[2].astype(F32),
        cross_ref[2].astype(F32),
        odd,
    )
    raw_ref[...] = tokens.astype(BF16)
    normed = rms_scaled(tokens, gain_ref[...]).astype(BF16)
    rows = (dot(normed, wq_ref[...]) * (1.0 / math.sqrt(channels))).astype(BF16)
    keys_ref[...] = dot_t(rows, wk_ref[...]).astype(BF16)


def lanes(value, width):
    return jnp.broadcast_to(value, (value.shape[0], width))


def key_rows(refs, gain):
    parts = [
        rms_scaled(ref[...].reshape(-1, gain.shape[1]).astype(F32), gain).astype(BF16) for ref in refs
    ]
    return parts[0] if len(parts) == 1 else jnp.concatenate(parts, axis=0)


def fold_kernel(blocks, first, gain_ref, own_ref, twin_ref, *refs):
    keys = key_rows(refs[:blocks], gain_ref[...])
    states, outs = ((None, None), refs[blocks:]) if first else (refs[blocks:-2], refs[-2:])
    channels = keys.shape[1]
    length = own_ref.shape[0]
    all_scores = dot_t(jnp.concatenate([own_ref[...], twin_ref[...]], axis=0), keys)
    peaks, totals, weights = [], [], []
    for k, state in enumerate(states):
        scores = all_scores[k * length : (k + 1) * length]
        peak = jnp.max(scores, axis=1, keepdims=True)
        if not first:
            peak = jnp.maximum(peak, state[:, channels : channels + 1])
        part = jnp.exp(scores - peak)
        peaks.append(peak)
        totals.append(jnp.sum(part, axis=1, keepdims=True))
        weights.append(part.astype(BF16))
    all_summed = dot(jnp.concatenate(weights, axis=0), keys)
    for k, (state, out) in enumerate(zip(states, outs)):
        summed, total, peak = all_summed[k * length : (k + 1) * length], totals[k], peaks[k]
        if not first:
            fade = jnp.exp(state[:, channels : channels + 1] - peak)
            total = total + fade * state[:, channels + 128 : channels + 129]
            summed = summed + fade * state[:, :channels]
        out[:, :channels] = summed
        out[:, channels : channels + 128] = lanes(peak, 128)
        out[:, channels + 128 :] = lanes(total, 128)


def fold(states, own, twin, gain, blocks):
    length, channels = own.shape
    shape = ((length, channels + 256), F32)
    first = states is None
    args = (gain, own, twin, *blocks, *(() if first else states))
    return call(functools.partial(fold_kernel, len(blocks), first), [shape, shape], args, 24 << 20)


def fetch_kernel(*refs):
    sems = refs[-1]
    sources, targets = refs[: len(refs) // 2], refs[len(refs) // 2 : -1]
    copies = [
        pltpu.make_async_copy(source, target, sems.at[k])
        for k, (source, target) in enumerate(zip(sources, targets))
    ]
    for copy in copies:
        copy.start()
    for copy in copies:
        copy.wait()


def finish_kernel(
    height, state_ref, other_ref, query_ref, last_ref, key_gain_ref, raw_ref, partial_ref,
    wv_ref, wo_ref, gain_ref, bias_ref, w_ref, hidden_ref, mixed_ref,
):
    length, channels = raw_ref.shape
    count, out = partial_ref.shape
    slots = edge_slots(count // height)
    row = lax.axis_index("rows")
    col = lax.axis_index("cols")
    has_top, has_bottom = row > 0, row < lax.axis_size("rows") - 1
    has_left, has_right = col > 0, col < lax.axis_size("cols") - 1

    keys = key_rows((last_ref,), key_gain_ref[...])
    scores = dot_t(query_ref[...], keys)
    peak_a, peak_b = state_ref[:, channels : channels + 1], other_ref[:, channels : channels + 1]
    peak = jnp.maximum(jnp.maximum(peak_a, peak_b), jnp.max(scores, axis=1, keepdims=True))
    fade_a, fade_b = jnp.exp(peak_a - peak), jnp.exp(peak_b - peak)
    weights = jnp.exp(scores - peak)
    total = jnp.sum(weights, axis=1, keepdims=True)
    total = total + fade_a * state_ref[:, channels + 128 : channels + 129]
    total = total + fade_b * other_ref[:, channels + 128 : channels + 129]
    summed = dot(weights.astype(BF16), keys)
    summed = summed + fade_a * state_ref[:, :channels] + fade_b * other_ref[:, :channels]
    pooled = (summed / total).astype(BF16)
    attended = dot(pooled, wv_ref[...]).astype(BF16)
    hidden = (raw_ref[...].astype(F32) + dot(attended, wo_ref[...])).astype(BF16)
    wide = hidden.astype(F32)
    value = rms_scaled(wide, gain_ref[...])
    value = value / (1.0 + jnp.exp(-value))
    slot = lax.broadcasted_iota(jnp.int32, (length, 1), 0)
    main_end = length - slots
    width = count // height
    in_top, in_bottom = slot < slots, slot >= main_end
    in_left = (slot >= slots) & (slot < slots + height)
    in_right = (slot >= main_end - height) & (slot < main_end)
    in_left = in_left | (slot == slots - 1) | (slot == length - 1)
    in_right = in_right | (slot == width) | (slot == main_end + width)
    outside = (in_top & jnp.logical_not(has_top)) | (in_bottom & jnp.logical_not(has_bottom))
    outside = outside | (in_left & jnp.logical_not(has_left)) | (in_right & jnp.logical_not(has_right))
    ext = jnp.where(outside, 0.0, value).astype(BF16)

    own = hidden[slots + height : slots + height + count]
    hidden_ref[...] = own
    result = partial_ref[...] + own[:, :out].astype(F32) + bias_ref[...]
    for i in range(3):
        lo, hi = conv_rows(length, slots, i)
        sums = None
        for j in range(3):
            sums = add_taps(sums, dot(ext[lo:hi], w_ref[2, i, j]), i, j, height, count)
        result = result + shifted_rows(sums, i, height)
    mixed_ref[...] = result.astype(BF16)


def join_kernel(a_ref, b_ref, out_ref):
    count = b_ref.shape[0]
    out_ref[:count] = a_ref[...].reshape(b_ref.shape)
    out_ref[count:] = b_ref[...]


def narrow(cols):
    return cols == 4


def moved(value, pairs):
    return lax.ppermute(value, AXES, pairs)


def block(
    frame_in, norm_gain, w_query, w_key, w_value, w_out, conv_gain, conv_cache, w_conv, conv_bias
):
    height, width, channels = frame_in.shape
    out_channels = w_conv.shape[4]
    count = height * width
    chips, ring, twin_pairs, down, up, cross_pairs = permutations(
        lax.axis_size("rows"), lax.axis_size("cols")
    )
    frame_far = jnp.transpose(frame_in, (1, 0, 2))
    cache_far = jnp.transpose(conv_cache, (0, 2, 1, 3))
    gain_far = norm_gain.reshape(1, channels)

    rows = edge_rows(width)
    tiles = [(frame_far.shape, BF16), (cache_far.shape, BF16), (gain_far.shape, F32)]
    far_tiles = (frame_far, cache_far, gain_far)
    edge = ((3, rows, channels), BF16)
    side = ((3, side_slots(height), channels), BF16)
    pair = ((2 * count, channels), BF16)
    sems = [pltpu.SemaphoreType.DMA((3,))]
    hops = (chips - 1) // 2
    if narrow(lax.axis_size("cols")):
        frame, cache, gain, edges, to_partner = call(
            pack_swap_kernel,
            tiles + [((2 * rows, channels), BF16), ((count + 2 * (rows + height), channels), BF16)],
            (), far_args=far_tiles, scratch=sems,
        )
        partner = moved(to_partner, twin_pairs)
        (first_hop,) = call(join_edges_kernel, [((2 * count + 4 * rows, channels), BF16)], (frame, edges, partner))
        arrived = moved(first_hop, ring)
        chain, mine = call(functools.partial(split_kernel, height), [pair, ((6 * rows, channels), BF16)], (arrived,))
        theirs = moved(mine, twin_pairs)
        top, bottom, twin, to_cross = call(
            sort_edges_kernel, [edge, edge, side, side], (frame, cache, partner, mine, theirs)
        )
    else:
        frame, cache, gain, first_rows, last_rows = call(
            pack_rows_kernel, tiles + [edge, edge], (), far_args=far_tiles, scratch=sems
        )
        partner = moved(frame_far.reshape(count, channels), twin_pairs)
        (chain,) = call(join_kernel, [pair], (frame, partner))
        chain = moved(chain, ring)
        top = moved(last_rows, down)
        bottom = moved(first_rows, up)
        to_twin, to_cross = call(pack_cols_kernel, [side, side], (frame, cache, top, bottom))
        twin = moved(to_twin, twin_pairs)
    cross = moved(to_cross, cross_pairs)
    blocks = [frame, chain]
    for _ in range(1, hops):
        chain = moved(chain, ring)
        blocks.append(chain)
    last = moved(chain, ring)

    far_args = (
        w_query, w_key, w_value, w_out, conv_gain.reshape(1, channels),
        conv_bias.reshape(1, out_channels), w_conv,
    )
    w_query, w_key, w_value, w_out, conv_gain, conv_bias, w_conv = call(
        fetch_kernel, [(a.shape, a.dtype) for a in far_args], (),
        far_args=far_args, scratch=[pltpu.SemaphoreType.DMA((len(far_args),))],
    )
    ext = ((2 * edge_slots(width) + (width + 2) * height, channels), BF16)
    raw, queries = call(query_kernel, [ext, ext], (frame, top, bottom, twin, cross, gain, w_query, w_key))
    twin_queries = moved(queries, twin_pairs)
    (partial,) = call(cache_conv_kernel, [((count, out_channels), F32)], (cache, top, bottom, twin, cross, w_conv))
    states = None
    for k in range(0, len(blocks), 4):
        states = fold(states, queries, twin_queries, gain, blocks[k : k + 4])
    other = moved(states[1], twin_pairs)
    hidden, mixed = call(
        functools.partial(finish_kernel, height),
        [((count, channels), BF16), ((count, out_channels), BF16)],
        (
            states[0], other, queries, last, gain, raw, partial, w_value, w_out, conv_gain, conv_bias,
            w_conv,
        ),
        24 << 20,
        far=True,
    )
    hidden = jnp.transpose(hidden.reshape(width, height, channels), (1, 0, 2))
    mixed = jnp.transpose(mixed.reshape(width, height, out_channels), (1, 0, 2))
    return (hidden, mixed)


def solution(mesh):
    in_specs = (
        P(("video", "rows"), "cols", None),
        P(),
        P(),
        P(),
        P(),
        P(),
        P(),
        P(None, ("video", "rows"), "cols", None),
        P(),
        P(),
    )
    out_specs = (P(("video", "rows"), "cols", None), P(("video", "rows"), "cols", None))
    return jax.shard_map(block, mesh=mesh, in_specs=in_specs, out_specs=out_specs, check_vma=False)
```

```python
import functools
import math

import jax
import jax.numpy as jnp
from jax import lax
from jax.experimental import pallas as pl
from jax.experimental.pallas import tpu as pltpu
from jax.sharding import PartitionSpec as P


EPS = 1e-06
AXES = ("rows", "cols")
F32 = jnp.float32
COST = 2_000_000_000
BF16 = jnp.bfloat16
VM = pl.BlockSpec(memory_space=pltpu.VMEM)


def near(value):
    return pltpu.with_memory_space_constraint(value, pltpu.VMEM)


def call(kernel, outs, args, limit=16 << 20, far_args=(), far=False, scratch=()):
    return pl.pallas_call(
        kernel,
        in_specs=[VM] * len(args) + [pl.BlockSpec(memory_space=pltpu.HBM)] * len(far_args),
        out_specs=[VM] * len(outs),
        out_shape=[
            jax.ShapeDtypeStruct(shape, dtype) if far else pltpu.VMEM(shape, dtype)
            for shape, dtype in outs
        ],
        scratch_shapes=scratch,
        compiler_params=pltpu.CompilerParams(vmem_limit_bytes=limit),
        cost_estimate=pl.CostEstimate(flops=COST, bytes_accessed=4 << 20, transcendentals=0),
    )(*[near(a) for a in args], *[pltpu.with_memory_space_constraint(a, pltpu.HBM) for a in far_args])


def chip_cycle(height, width):
    if width == 1 or height == 1:
        return [(z, x) for z in range(height) for x in range(width)]
    order = []
    for x in range(width):
        inner = range(1, height) if x % 2 == 0 else range(height - 1, 0, -1)
        order += [(z, x) for z in inner]
    return order + [(0, x) for x in range(width - 1, -1, -1)]


def permutations(rows, cols):
    def at(z, x, core):
        return z * cols + 2 * x + core

    walk = chip_cycle(rows, cols // 2)
    ring = []
    for k, here in enumerate(walk):
        there = walk[(k + 1) % len(walk)]
        ring += [(at(*here, 0), at(*there, 0)), (at(*there, 1), at(*here, 1))]
    twin = [(i, i ^ 1) for i in range(rows * cols)]
    down = [(i, i + cols) for i in range((rows - 1) * cols)]
    up = [(j, i) for i, j in down]
    cross = []
    for r in range(rows):
        for c in range(1, cols - 1, 2):
            i = r * cols + c
            cross += [(i, i + 1), (i + 1, i)]
    return len(walk), ring, twin, down, up, cross


def edge_slots(width):
    return -(-(width + 2) // 16) * 16


def edge_rows(width):
    return -(-width // 8) * 8


def side_slots(height):
    return height + 8


def rms_scaled(values, gain):
    mean_sq = jnp.mean(values * values, axis=-1, keepdims=True)
    return values * lax.rsqrt(mean_sq + EPS) * gain


def dot(a, b):
    return jnp.dot(a, b, preferred_element_type=F32)


def dot_t(a, b):
    return lax.dot_general(a, b, (((1,), (1,)), ((), ())), preferred_element_type=F32)


def row_edge(tile, r):
    width, _, channels = tile.shape
    fill = jnp.zeros((edge_rows(width) - width, channels), F32)
    return jnp.concatenate([tile[c, r : r + 1, :] for c in range(width)] + [fill], axis=0)


def load_tiles(frame_hbm, cache_hbm, gain_hbm, frame_ref, cache_ref, gain_ref, sems):
    copies = [
        pltpu.make_async_copy(frame_hbm, frame_ref, sems.at[0]),
        pltpu.make_async_copy(cache_hbm, cache_ref, sems.at[1]),
        pltpu.make_async_copy(gain_hbm, gain_ref, sems.at[2]),
    ]
    for copy in copies:
        copy.start()
    for copy in copies:
        copy.wait()


def pack_rows_kernel(frame_hbm, cache_hbm, gain_hbm, frame_ref, cache_ref, gain_ref, first_ref, last_ref, sems):
    load_tiles(frame_hbm, cache_hbm, gain_hbm, frame_ref, cache_ref, gain_ref, sems)
    height = frame_ref.shape[1]
    for t in range(3):
        tile = (frame_ref[...] if t == 2 else cache_ref[t]).astype(F32)
        first_ref[t] = row_edge(tile, 0).astype(BF16)
        last_ref[t] = row_edge(tile, height - 1).astype(BF16)


def faces_up():
    col = lax.axis_index("cols")
    return lax.rem(lax.rem(col, 2) + lax.div(col, 2), 2)


def pack_chain_kernel(frame_hbm, cache_hbm, gain_hbm, frame_ref, cache_ref, gain_ref, chain_ref, swap_ref, sems):
    load_tiles(frame_hbm, cache_hbm, gain_hbm, frame_ref, cache_ref, gain_ref, sems)
    width, height, channels = frame_ref.shape
    count, rows = width * height, edge_rows(width)
    up = faces_up()
    chain_ref[:count] = frame_ref[...].reshape(count, channels)
    swap_ref[:count] = frame_ref[...].reshape(count, channels)
    for t in range(2):
        tile = cache_ref[t].astype(F32)
        first, last = row_edge(tile, 0), row_edge(tile, height - 1)
        at = count + t * rows
        chain_ref[at : at + rows] = jnp.where(up == 1, first, last).astype(BF16)
        swap_ref[at : at + rows] = jnp.where(up == 1, last, first).astype(BF16)


def cut_kernel(arrived_ref, chain_ref):
    chain_ref[...] = arrived_ref[: chain_ref.shape[0]]


def split_kernel(cache_ref, a_ref, b_ref, edges_ref):
    _, width, height, _ = cache_ref.shape
    count, rows = width * height, edge_rows(width)
    up = faces_up()
    odd = lax.rem(lax.axis_index("cols"), 2)
    for k, ref in enumerate((a_ref, b_ref)):
        to = k * 3 * rows
        edges_ref[to : to + 2 * rows] = ref[count : count + 2 * rows]
        tile = ref[:count].astype(F32).reshape(width, height, -1)
        edge = jnp.where(up == 1, row_edge(tile, 0), row_edge(tile, height - 1))
        edges_ref[to + 2 * rows : to + 3 * rows] = edge.astype(BF16)
    for t in range(2):
        at = 6 * rows + t * height
        column = jnp.where(odd == 1, cache_ref[t, 0].astype(F32), cache_ref[t, width - 1].astype(F32))
        edges_ref[at : at + height] = column.astype(BF16)


def sort_edges_kernel(
    frame_ref, cache_ref, partner_ref, mine_ref, theirs_ref, top_ref, bottom_ref, twin_ref, cross_ref
):
    width, height, channels = frame_ref.shape
    count, rows = width * height, top_ref.shape[1]
    up = faces_up()
    odd = lax.rem(lax.axis_index("cols"), 2)
    row = lax.axis_index("rows")
    has_top, has_bottom = row > 0, row < lax.axis_size("rows") - 1
    fill = jnp.zeros((side_slots(height) - height - 2, channels), F32)
    for t in range(3):
        pair = []
        for k in range(2):
            mine = mine_ref[(3 * k + t) * rows : (3 * k + t + 1) * rows].astype(F32)
            theirs = theirs_ref[(3 - 3 * k + t) * rows : (4 - 3 * k + t) * rows].astype(F32)
            top = jnp.where(has_top, jnp.where(up == 1, theirs, mine), 0.0)
            bottom = jnp.where(has_bottom, jnp.where(up == 1, mine, theirs), 0.0)
            pair.append((top, bottom))
        (top, bottom), (twin_top, twin_bottom) = pair
        top_ref[t] = top.astype(BF16)
        bottom_ref[t] = bottom.astype(BF16)

        def facing(first, value, axis_rows):
            a, b = value[axis_rows(0)], value[axis_rows(width - 1)]
            return jnp.where(first, a, b)

        if t == 2:
            block = partner_ref[:count].astype(F32)
            column = facing(odd == 0, block, lambda c: slice(c * height, (c + 1) * height))
        else:
            at = 6 * rows + t * height
            column = theirs_ref[at : at + height].astype(F32)
        corners = [facing(odd == 0, v, lambda c: slice(c, c + 1)) for v in (twin_top, twin_bottom)]
        twin_ref[t] = jnp.concatenate([column, *corners, fill], axis=0).astype(BF16)
        tile = (frame_ref[...] if t == 2 else cache_ref[t]).astype(F32)
        column = jnp.where(odd == 0, tile[0], tile[width - 1])
        corners = [facing(odd == 0, v, lambda c: slice(c, c + 1)) for v in (top, bottom)]
        cross_ref[t] = jnp.concatenate([column, *corners, fill], axis=0).astype(BF16)


def pack_cols_kernel(frame_ref, cache_ref, top_ref, bottom_ref, twin_ref, cross_ref):
    width, height, channels = frame_ref.shape
    odd = lax.rem(lax.axis_index("cols"), 2)
    fill = jnp.zeros((side_slots(height) - height - 2, channels), F32)
    for t in range(3):
        sides = []
        for c in (0, width - 1):
            own = (frame_ref[c] if t == 2 else cache_ref[t, c]).astype(F32)
            top = top_ref[t].astype(F32)[c : c + 1, :]
            bottom = bottom_ref[t].astype(F32)[c : c + 1, :]
            sides.append(jnp.concatenate([own, top, bottom, fill], axis=0))
        left, right = sides
        twin_ref[t] = jnp.where(odd == 1, left, right).astype(BF16)
        cross_ref[t] = jnp.where(odd == 1, right, left).astype(BF16)


def extended(own, top, bottom, twin, cross, odd):
    height = twin.shape[0] - side_slots(0)
    left = jnp.where(odd == 1, twin, cross)
    right = jnp.where(odd == 1, cross, twin)
    width = own.shape[0] // height
    slots = edge_slots(width)
    slot = lax.broadcasted_iota(jnp.int32, (slots, own.shape[1]), 0)
    fill = jnp.zeros((slots - top.shape[0], own.shape[1]), F32)

    def edge(row, k):
        row = jnp.concatenate([row, fill], axis=0)
        row = jnp.where(slot == width, right[k : k + 1, :], row)
        return jnp.where(slot == slots - 1, left[k : k + 1, :], row)

    return jnp.concatenate(
        [edge(top, height), left[:height], own, right[:height], edge(bottom, height + 1)], axis=0
    )


def conv_rows(ext_len, slots, i):
    return (0 if i == 0 else slots), (ext_len if i == 2 else ext_len - slots)


def add_taps(sums, products, i, j, height, count):
    slots = edge_slots(count // height)
    main = products[slots:] if i == 0 else products
    part = main[j * height : j * height + count]
    edge = None
    if i == 0:
        edge = products[:slots]
    if i == 2:
        edge = products[products.shape[0] - slots :]
    if edge is not None and j != 1:
        edge = pltpu.roll(edge, 1 if j == 0 else slots - 1, 0)
    if sums is None:
        return part, edge
    return sums[0] + part, (None if edge is None else sums[1] + edge)


def shifted_rows(sums, i, height):
    main, edge = sums
    if i == 1:
        return main
    count, out = main.shape
    width = count // height
    tile = main.reshape(width, height, out)
    moved = pltpu.roll(tile, 1 if i == 0 else height - 1, 1)
    row = lax.broadcasted_iota(jnp.int32, (height, out), 0)
    at = 0 if i == 0 else height - 1
    cells = [jnp.where(row == at, edge[c : c + 1, :], moved[c]) for c in range(width)]
    return jnp.concatenate(cells, axis=0)


def cache_conv_kernel(cache_ref, top_ref, bottom_ref, twin_ref, cross_ref, w_ref, out_ref):
    width, height, channels = cache_ref.shape[1:]
    count = width * height
    odd = lax.rem(lax.axis_index("cols"), 2)
    exts = [
        extended(
            cache_ref[t].reshape(count, channels).astype(F32),
            top_ref[t].astype(F32),
            bottom_ref[t].astype(F32),
            twin_ref[t].astype(F32),
            cross_ref[t].astype(F32),
            odd,
        ).astype(BF16)
        for t in range(2)
    ]
    result = None
    for i in range(3):
        lo, hi = conv_rows(exts[0].shape[0], edge_slots(width), i)
        sums = None
        for j in range(3):
            products = dot(exts[0][lo:hi], w_ref[0, i, j]) + dot(exts[1][lo:hi], w_ref[1, i, j])
            sums = add_taps(sums, products, i, j, height, count)
        value = shifted_rows(sums, i, height)
        result = value if result is None else result + value
    out_ref[...] = result


def query_kernel(
    frame_ref, top_ref, bottom_ref, twin_ref, cross_ref, gain_ref, wq_ref, wk_ref, raw_ref, keys_ref
):
    width, height, channels = frame_ref.shape
    odd = lax.rem(lax.axis_index("cols"), 2)
    tokens = extended(
        frame_ref[...].reshape(width * height, channels).astype(F32),
        top_ref[2].astype(F32),
        bottom_ref[2].astype(F32),
        twin_ref[2].astype(F32),
        cross_ref[2].astype(F32),
        odd,
    )
    raw_ref[...] = tokens.astype(BF16)
    normed = rms_scaled(tokens, gain_ref[...]).astype(BF16)
    rows = (dot(normed, wq_ref[...]) * (1.0 / math.sqrt(channels))).astype(BF16)
    keys_ref[...] = dot_t(rows, wk_ref[...]).astype(BF16)


def lanes(value, width):
    return jnp.broadcast_to(value, (value.shape[0], width))


def key_rows(refs, gain):
    parts = [
        rms_scaled(ref[...].reshape(-1, gain.shape[1]).astype(F32), gain).astype(BF16) for ref in refs
    ]
    return parts[0] if len(parts) == 1 else jnp.concatenate(parts, axis=0)


def fold_kernel(blocks, first, gain_ref, own_ref, twin_ref, *refs):
    keys = key_rows(refs[:blocks], gain_ref[...])
    states, outs = ((None, None), refs[blocks:]) if first else (refs[blocks:-2], refs[-2:])
    channels = keys.shape[1]
    length = own_ref.shape[0]
    all_scores = dot_t(jnp.concatenate([own_ref[...], twin_ref[...]], axis=0), keys)
    peaks, totals, weights = [], [], []
    for k, state in enumerate(states):
        scores = all_scores[k * length : (k + 1) * length]
        peak = jnp.max(scores, axis=1, keepdims=True)
        if not first:
            peak = jnp.maximum(peak, state[:, channels : channels + 1])
        part = jnp.exp(scores - peak)
        peaks.append(peak)
        totals.append(jnp.sum(part, axis=1, keepdims=True))
        weights.append(part.astype(BF16))
    all_summed = dot(jnp.concatenate(weights, axis=0), keys)
    for k, (state, out) in enumerate(zip(states, outs)):
        summed, total, peak = all_summed[k * length : (k + 1) * length], totals[k], peaks[k]
        if not first:
            fade = jnp.exp(state[:, channels : channels + 1] - peak)
            total = total + fade * state[:, channels + 128 : channels + 129]
            summed = summed + fade * state[:, :channels]
        out[:, :channels] = summed
        out[:, channels : channels + 128] = lanes(peak, 128)
        out[:, channels + 128 :] = lanes(total, 128)


def fold(states, own, twin, gain, blocks):
    length, channels = own.shape
    shape = ((length, channels + 256), F32)
    first = states is None
    args = (gain, own, twin, *blocks, *(() if first else states))
    return call(functools.partial(fold_kernel, len(blocks), first), [shape, shape], args, 24 << 20)


def finish_kernel(
    height, state_ref, other_ref, query_ref, last_a_ref, last_b_ref, key_gain_ref, raw_ref, partial_ref,
    wv_ref, wo_ref, gain_ref, bias_ref, w_ref, hidden_ref, mixed_ref,
):
    length, channels = raw_ref.shape
    count, out = partial_ref.shape
    slots = edge_slots(count // height)
    row = lax.axis_index("rows")
    col = lax.axis_index("cols")
    has_top, has_bottom = row > 0, row < lax.axis_size("rows") - 1
    has_left, has_right = col > 0, col < lax.axis_size("cols") - 1

    keys = key_rows((last_a_ref, last_b_ref), key_gain_ref[...])
    scores = dot_t(query_ref[...], keys)
    peak_a, peak_b = state_ref[:, channels : channels + 1], other_ref[:, channels : channels + 1]
    peak = jnp.maximum(jnp.maximum(peak_a, peak_b), jnp.max(scores, axis=1, keepdims=True))
    fade_a, fade_b = jnp.exp(peak_a - peak), jnp.exp(peak_b - peak)
    weights = jnp.exp(scores - peak)
    total = jnp.sum(weights, axis=1, keepdims=True)
    total = total + fade_a * state_ref[:, channels + 128 : channels + 129]
    total = total + fade_b * other_ref[:, channels + 128 : channels + 129]
    summed = dot(weights.astype(BF16), keys)
    summed = summed + fade_a * state_ref[:, :channels] + fade_b * other_ref[:, :channels]
    pooled = (summed / total).astype(BF16)
    attended = dot(pooled, wv_ref[...]).astype(BF16)
    hidden = (raw_ref[...].astype(F32) + dot(attended, wo_ref[...])).astype(BF16)
    wide = hidden.astype(F32)
    value = rms_scaled(wide, gain_ref[...])
    value = value / (1.0 + jnp.exp(-value))
    slot = lax.broadcasted_iota(jnp.int32, (length, 1), 0)
    main_end = length - slots
    width = count // height
    in_top, in_bottom = slot < slots, slot >= main_end
    in_left = (slot >= slots) & (slot < slots + height)
    in_right = (slot >= main_end - height) & (slot < main_end)
    in_left = in_left | (slot == slots - 1) | (slot == length - 1)
    in_right = in_right | (slot == width) | (slot == main_end + width)
    outside = (in_top & jnp.logical_not(has_top)) | (in_bottom & jnp.logical_not(has_bottom))
    outside = outside | (in_left & jnp.logical_not(has_left)) | (in_right & jnp.logical_not(has_right))
    ext = jnp.where(outside, 0.0, value).astype(BF16)

    own = hidden[slots + height : slots + height + count]
    hidden_ref[...] = own
    result = partial_ref[...] + own[:, :out].astype(F32) + bias_ref[...]
    for i in range(3):
        lo, hi = conv_rows(length, slots, i)
        sums = None
        for j in range(3):
            sums = add_taps(sums, dot(ext[lo:hi], w_ref[2, i, j]), i, j, height, count)
        result = result + shifted_rows(sums, i, height)
    mixed_ref[...] = result.astype(BF16)


def narrow(cols):
    return cols == 4


def moved(value, pairs):
    return lax.ppermute(value, AXES, pairs)


def block(
    frame_in, norm_gain, w_query, w_key, w_value, w_out, conv_gain, conv_cache, w_conv, conv_bias
):
    height, width, channels = frame_in.shape
    out_channels = w_conv.shape[4]
    count = height * width
    chips, ring, twin_pairs, down, up, cross_pairs = permutations(
        lax.axis_size("rows"), lax.axis_size("cols")
    )
    frame_far = jnp.transpose(frame_in, (1, 0, 2))
    cache_far = jnp.transpose(conv_cache, (0, 2, 1, 3))
    gain_far = norm_gain.reshape(1, channels)

    rows = edge_rows(width)
    tiles = [(frame_far.shape, BF16), (cache_far.shape, BF16), (gain_far.shape, F32)]
    far_tiles = (frame_far, cache_far, gain_far)
    edge = ((3, rows, channels), BF16)
    side = ((3, side_slots(height), channels), BF16)
    keys = ((count, channels), BF16)
    sems = [pltpu.SemaphoreType.DMA((3,))]
    hops = (chips - 1) // 2
    if narrow(lax.axis_size("cols")):
        with_row = ((count + 2 * rows, channels), BF16)
        frame, cache, gain, chain_a, to_partner = call(
            pack_chain_kernel, tiles + [with_row, with_row], (), far_args=far_tiles, scratch=sems
        )
        partner = moved(to_partner, twin_pairs)
        arrived_a = moved(chain_a, ring)
        arrived_b = moved(partner, ring)
        (chain_a,) = call(cut_kernel, [keys], (arrived_a,))
        (chain_b,) = call(cut_kernel, [keys], (arrived_b,))
        (mine,) = call(split_kernel, [((6 * rows + 2 * height, channels), BF16)], (cache, arrived_a, arrived_b))
        theirs = moved(mine, twin_pairs)
        top, bottom, twin, to_cross = call(
            sort_edges_kernel, [edge, edge, side, side], (frame, cache, partner, mine, theirs)
        )
    else:
        frame, cache, gain, first_rows, last_rows = call(
            pack_rows_kernel, tiles + [edge, edge], (), far_args=far_tiles, scratch=sems
        )
        chain_a = frame_far.reshape(count, channels)
        chain_b = moved(chain_a, twin_pairs)
        chain_a = moved(chain_a, ring)
        chain_b = moved(chain_b, ring)
        top = moved(last_rows, down)
        bottom = moved(first_rows, up)
        to_twin, to_cross = call(pack_cols_kernel, [side, side], (frame, cache, top, bottom))
        twin = moved(to_twin, twin_pairs)
    cross = moved(to_cross, cross_pairs)
    blocks = [frame, chain_a, chain_b]
    for _ in range(1, hops):
        chain_a = moved(chain_a, ring)
        chain_b = moved(chain_b, ring)
        blocks += [chain_a, chain_b]
    last_a = moved(chain_a, ring)
    last_b = moved(chain_b, ring)

    far_args = (
        w_query, w_key, w_value, w_out, conv_gain.reshape(1, channels),
        conv_bias.reshape(1, out_channels), w_conv,
    )
    w_query, w_key, w_value, w_out, conv_gain, conv_bias, w_conv = far_args
    ext = ((2 * edge_slots(width) + (width + 2) * height, channels), BF16)
    raw, queries = call(query_kernel, [ext, ext], (frame, top, bottom, twin, cross, gain, w_query, w_key))
    twin_queries = moved(queries, twin_pairs)
    (partial,) = call(cache_conv_kernel, [((count, out_channels), F32)], (cache, top, bottom, twin, cross, w_conv))
    states = None
    for k in range(0, len(blocks), 7):
        states = fold(states, queries, twin_queries, gain, blocks[k : k + 7])
    other = moved(states[1], twin_pairs)
    hidden, mixed = call(
        functools.partial(finish_kernel, height),
        [((count, channels), BF16), ((count, out_channels), BF16)],
        (
            states[0], other, queries, last_a, last_b, gain, raw, partial, w_value, w_out, conv_gain, conv_bias,
            w_conv,
        ),
        24 << 20,
        far=True,
    )
    hidden = jnp.transpose(hidden.reshape(width, height, channels), (1, 0, 2))
    mixed = jnp.transpose(mixed.reshape(width, height, out_channels), (1, 0, 2))
    return (hidden, mixed)


def solution(mesh):
    in_specs = (
        P(("video", "rows"), "cols", None),
        P(),
        P(),
        P(),
        P(),
        P(),
        P(),
        P(None, ("video", "rows"), "cols", None),
        P(),
        P(),
    )
    out_specs = (P(("video", "rows"), "cols", None), P(("video", "rows"), "cols", None))
    return jax.shard_map(block, mesh=mesh, in_specs=in_specs, out_specs=out_specs, check_vma=False)
```

```python
import functools
import math

import jax
import jax.numpy as jnp
from jax import lax
from jax.experimental import pallas as pl
from jax.experimental.pallas import tpu as pltpu
from jax.sharding import PartitionSpec as P


EPS = 1e-06
AXES = ("rows", "cols")
F32 = jnp.float32
COST = 2_000_000_000
BF16 = jnp.bfloat16
VM = pl.BlockSpec(memory_space=pltpu.VMEM)


def near(value):
    return pltpu.with_memory_space_constraint(value, pltpu.VMEM)


def call(kernel, outs, args, limit=16 << 20, far_args=(), far=False, scratch=()):
    return pl.pallas_call(
        kernel,
        in_specs=[VM] * len(args) + [pl.BlockSpec(memory_space=pltpu.HBM)] * len(far_args),
        out_specs=[VM] * len(outs),
        out_shape=[
            jax.ShapeDtypeStruct(shape, dtype) if far else pltpu.VMEM(shape, dtype)
            for shape, dtype in outs
        ],
        scratch_shapes=scratch,
        compiler_params=pltpu.CompilerParams(vmem_limit_bytes=limit),
        cost_estimate=pl.CostEstimate(flops=COST, bytes_accessed=4 << 20, transcendentals=0),
    )(*[near(a) for a in args], *[pltpu.with_memory_space_constraint(a, pltpu.HBM) for a in far_args])


def chip_cycle(height, width):
    if width == 1 or height == 1:
        return [(z, x) for z in range(height) for x in range(width)]
    order = []
    for x in range(width):
        inner = range(1, height) if x % 2 == 0 else range(height - 1, 0, -1)
        order += [(z, x) for z in inner]
    return order + [(0, x) for x in range(width - 1, -1, -1)]


def permutations(rows, cols):
    def at(z, x, core):
        return z * cols + 2 * x + core

    walk = chip_cycle(rows, cols // 2)
    ring = []
    for k, here in enumerate(walk):
        there = walk[(k + 1) % len(walk)]
        ring += [(at(*here, 0), at(*there, 0)), (at(*there, 1), at(*here, 1))]
    twin = [(i, i ^ 1) for i in range(rows * cols)]
    down = [(i, i + cols) for i in range((rows - 1) * cols)]
    up = [(j, i) for i, j in down]
    cross = []
    for r in range(rows):
        for c in range(1, cols - 1, 2):
            i = r * cols + c
            cross += [(i, i + 1), (i + 1, i)]
    return len(walk), ring, twin, down, up, cross


def edge_slots(width):
    return -(-(width + 2) // 16) * 16


def edge_rows(width):
    return -(-width // 8) * 8


def side_slots(height):
    return height + 8


def rms_scaled(values, gain):
    mean_sq = jnp.mean(values * values, axis=-1, keepdims=True)
    return values * lax.rsqrt(mean_sq + EPS) * gain


def dot(a, b):
    return jnp.dot(a, b, preferred_element_type=F32)


def dot_t(a, b):
    return lax.dot_general(a, b, (((1,), (1,)), ((), ())), preferred_element_type=F32)


def row_edge(tile, r):
    width, _, channels = tile.shape
    fill = jnp.zeros((edge_rows(width) - width, channels), F32)
    return jnp.concatenate([tile[c, r : r + 1, :] for c in range(width)] + [fill], axis=0)


def load_tiles(frame_hbm, cache_hbm, gain_hbm, frame_ref, cache_ref, gain_ref, sems):
    copies = [
        pltpu.make_async_copy(frame_hbm, frame_ref, sems.at[0]),
        pltpu.make_async_copy(cache_hbm, cache_ref, sems.at[1]),
        pltpu.make_async_copy(gain_hbm, gain_ref, sems.at[2]),
    ]
    for copy in copies:
        copy.start()
    for copy in copies:
        copy.wait()


def pack_rows_kernel(frame_hbm, cache_hbm, gain_hbm, frame_ref, cache_ref, gain_ref, first_ref, last_ref, sems):
    load_tiles(frame_hbm, cache_hbm, gain_hbm, frame_ref, cache_ref, gain_ref, sems)
    height = frame_ref.shape[1]
    for t in range(3):
        tile = (frame_ref[...] if t == 2 else cache_ref[t]).astype(F32)
        first_ref[t] = row_edge(tile, 0).astype(BF16)
        last_ref[t] = row_edge(tile, height - 1).astype(BF16)


def faces_up():
    col = lax.axis_index("cols")
    return lax.rem(lax.rem(col, 2) + lax.div(col, 2), 2)


def pack_chain_kernel(frame_hbm, cache_hbm, gain_hbm, frame_ref, cache_ref, gain_ref, chain_ref, swap_ref, sems):
    load_tiles(frame_hbm, cache_hbm, gain_hbm, frame_ref, cache_ref, gain_ref, sems)
    width, height, channels = frame_ref.shape
    count, rows = width * height, edge_rows(width)
    up = faces_up()
    chain_ref[:count] = frame_ref[...].reshape(count, channels)
    swap_ref[:count] = frame_ref[...].reshape(count, channels)
    for t in range(2):
        tile = cache_ref[t].astype(F32)
        first, last = row_edge(tile, 0), row_edge(tile, height - 1)
        at = count + t * rows
        chain_ref[at : at + rows] = jnp.where(up == 1, first, last).astype(BF16)
        swap_ref[at : at + rows] = jnp.where(up == 1, last, first).astype(BF16)


def cut_kernel(arrived_ref, chain_ref):
    chain_ref[...] = arrived_ref[: chain_ref.shape[0]]


def split_kernel(cache_ref, a_ref, b_ref, edges_ref):
    _, width, height, _ = cache_ref.shape
    count, rows = width * height, edge_rows(width)
    up = faces_up()
    odd = lax.rem(lax.axis_index("cols"), 2)
    for k, ref in enumerate((a_ref, b_ref)):
        to = k * 3 * rows
        edges_ref[to : to + 2 * rows] = ref[count : count + 2 * rows]
        tile = ref[:count].astype(F32).reshape(width, height, -1)
        edge = jnp.where(up == 1, row_edge(tile, 0), row_edge(tile, height - 1))
        edges_ref[to + 2 * rows : to + 3 * rows] = edge.astype(BF16)
    for t in range(2):
        at = 6 * rows + t * height
        column = jnp.where(odd == 1, cache_ref[t, 0].astype(F32), cache_ref[t, width - 1].astype(F32))
        edges_ref[at : at + height] = column.astype(BF16)


def sort_edges_kernel(
    frame_ref, cache_ref, partner_ref, mine_ref, theirs_ref, top_ref, bottom_ref, twin_ref, cross_ref
):
    width, height, channels = frame_ref.shape
    count, rows = width * height, top_ref.shape[1]
    up = faces_up()
    odd = lax.rem(lax.axis_index("cols"), 2)
    row = lax.axis_index("rows")
    has_top, has_bottom = row > 0, row < lax.axis_size("rows") - 1
    fill = jnp.zeros((side_slots(height) - height - 2, channels), F32)
    for t in range(3):
        pair = []
        for k in range(2):
            mine = mine_ref[(3 * k + t) * rows : (3 * k + t + 1) * rows].astype(F32)
            theirs = theirs_ref[(3 - 3 * k + t) * rows : (4 - 3 * k + t) * rows].astype(F32)
            top = jnp.where(has_top, jnp.where(up == 1, theirs, mine), 0.0)
            bottom = jnp.where(has_bottom, jnp.where(up == 1, mine, theirs), 0.0)
            pair.append((top, bottom))
        (top, bottom), (twin_top, twin_bottom) = pair
        top_ref[t] = top.astype(BF16)
        bottom_ref[t] = bottom.astype(BF16)

        def facing(first, value, axis_rows):
            a, b = value[axis_rows(0)], value[axis_rows(width - 1)]
            return jnp.where(first, a, b)

        if t == 2:
            block = partner_ref[:count].astype(F32)
            column = facing(odd == 0, block, lambda c: slice(c * height, (c + 1) * height))
        else:
            at = 6 * rows + t * height
            column = theirs_ref[at : at + height].astype(F32)
        corners = [facing(odd == 0, v, lambda c: slice(c, c + 1)) for v in (twin_top, twin_bottom)]
        twin_ref[t] = jnp.concatenate([column, *corners, fill], axis=0).astype(BF16)
        tile = (frame_ref[...] if t == 2 else cache_ref[t]).astype(F32)
        column = jnp.where(odd == 0, tile[0], tile[width - 1])
        corners = [facing(odd == 0, v, lambda c: slice(c, c + 1)) for v in (top, bottom)]
        cross_ref[t] = jnp.concatenate([column, *corners, fill], axis=0).astype(BF16)


def pack_cols_kernel(frame_ref, cache_ref, top_ref, bottom_ref, twin_ref, cross_ref):
    width, height, channels = frame_ref.shape
    odd = lax.rem(lax.axis_index("cols"), 2)
    fill = jnp.zeros((side_slots(height) - height - 2, channels), F32)
    for t in range(3):
        sides = []
        for c in (0, width - 1):
            own = (frame_ref[c] if t == 2 else cache_ref[t, c]).astype(F32)
            top = top_ref[t].astype(F32)[c : c + 1, :]
            bottom = bottom_ref[t].astype(F32)[c : c + 1, :]
            sides.append(jnp.concatenate([own, top, bottom, fill], axis=0))
        left, right = sides
        twin_ref[t] = jnp.where(odd == 1, left, right).astype(BF16)
        cross_ref[t] = jnp.where(odd == 1, right, left).astype(BF16)


def extended(own, top, bottom, twin, cross, odd):
    height = twin.shape[0] - side_slots(0)
    left = jnp.where(odd == 1, twin, cross)
    right = jnp.where(odd == 1, cross, twin)
    width = own.shape[0] // height
    slots = edge_slots(width)
    slot = lax.broadcasted_iota(jnp.int32, (slots, own.shape[1]), 0)
    fill = jnp.zeros((slots - top.shape[0], own.shape[1]), F32)

    def edge(row, k):
        row = jnp.concatenate([row, fill], axis=0)
        row = jnp.where(slot == width, right[k : k + 1, :], row)
        return jnp.where(slot == slots - 1, left[k : k + 1, :], row)

    return jnp.concatenate(
        [edge(top, height), left[:height], own, right[:height], edge(bottom, height + 1)], axis=0
    )


def tap_rows(tokens, height, count):
    slots = edge_slots(count // height)
    main = tokens[slots : tokens.shape[0] - slots]
    mains = [main[j * height : j * height + count] for j in range(3)]
    result = []
    for edge in (tokens[:slots], None, tokens[tokens.shape[0] - slots :]):
        if edge is None:
            parts = mains
        else:
            edges = [pltpu.roll(edge, 1, 0), edge, pltpu.roll(edge, slots - 1, 0)]
            parts = [jnp.concatenate(pair, axis=0) for pair in zip(mains, edges)]
        result.append(jnp.concatenate([p.astype(BF16) for p in parts], axis=1))
    return result


def shifted_rows(sums, i, height, count):
    if i == 1:
        return sums
    main, edge = sums[:count], sums[count:]
    out = main.shape[1]
    width = count // height
    tile = main.reshape(width, height, out)
    moved = pltpu.roll(tile, 1 if i == 0 else height - 1, 1)
    row = lax.broadcasted_iota(jnp.int32, (height, out), 0)
    at = 0 if i == 0 else height - 1
    cells = [jnp.where(row == at, edge[c : c + 1, :], moved[c]) for c in range(width)]
    return jnp.concatenate(cells, axis=0)


def cache_conv_kernel(cache_ref, top_ref, bottom_ref, twin_ref, cross_ref, w_ref, out_ref):
    width, height, channels = cache_ref.shape[1:]
    count = width * height
    odd = lax.rem(lax.axis_index("cols"), 2)
    rows = [
        tap_rows(
            extended(
                cache_ref[t].reshape(count, channels).astype(F32),
                top_ref[t].astype(F32),
                bottom_ref[t].astype(F32),
                twin_ref[t].astype(F32),
                cross_ref[t].astype(F32),
                odd,
            ),
            height,
            count,
        )
        for t in range(2)
    ]
    result = None
    for i in range(3):
        patches = jnp.concatenate([rows[0][i], rows[1][i]], axis=1)
        taps = w_ref[:2, i].reshape(-1, w_ref.shape[4])
        value = shifted_rows(dot(patches, taps), i, height, count)
        result = value if result is None else result + value
    out_ref[...] = result


def query_kernel(
    frame_ref, top_ref, bottom_ref, twin_ref, cross_ref, gain_ref, wq_ref, wk_ref, raw_ref, keys_ref
):
    width, height, channels = frame_ref.shape
    odd = lax.rem(lax.axis_index("cols"), 2)
    tokens = extended(
        frame_ref[...].reshape(width * height, channels).astype(F32),
        top_ref[2].astype(F32),
        bottom_ref[2].astype(F32),
        twin_ref[2].astype(F32),
        cross_ref[2].astype(F32),
        odd,
    )
    raw_ref[...] = tokens.astype(BF16)
    normed = rms_scaled(tokens, gain_ref[...]).astype(BF16)
    rows = (dot(normed, wq_ref[...]) * (1.0 / math.sqrt(channels))).astype(BF16)
    keys_ref[...] = dot_t(rows, wk_ref[...]).astype(BF16)


def lanes(value, width):
    return jnp.broadcast_to(value, (value.shape[0], width))


def key_rows(refs, gain):
    parts = [
        rms_scaled(ref[...].reshape(-1, gain.shape[1]).astype(F32), gain).astype(BF16) for ref in refs
    ]
    return parts[0] if len(parts) == 1 else jnp.concatenate(parts, axis=0)


def fold_kernel(blocks, first, gain_ref, own_ref, twin_ref, *refs):
    keys = key_rows(refs[:blocks], gain_ref[...])
    states, outs = ((None, None), refs[blocks:]) if first else (refs[blocks:-2], refs[-2:])
    channels = keys.shape[1]
    length = own_ref.shape[0]
    all_scores = dot_t(jnp.concatenate([own_ref[...], twin_ref[...]], axis=0), keys)
    peaks, totals, weights = [], [], []
    for k, state in enumerate(states):
        scores = all_scores[k * length : (k + 1) * length]
        peak = jnp.max(scores, axis=1, keepdims=True)
        if not first:
            peak = jnp.maximum(peak, state[:, channels : channels + 1])
        part = jnp.exp(scores - peak)
        peaks.append(peak)
        totals.append(jnp.sum(part, axis=1, keepdims=True))
        weights.append(part.astype(BF16))
    all_summed = dot(jnp.concatenate(weights, axis=0), keys)
    for k, (state, out) in enumerate(zip(states, outs)):
        summed, total, peak = all_summed[k * length : (k + 1) * length], totals[k], peaks[k]
        if not first:
            fade = jnp.exp(state[:, channels : channels + 1] - peak)
            total = total + fade * state[:, channels + 128 : channels + 129]
            summed = summed + fade * state[:, :channels]
        out[:, :channels] = summed
        out[:, channels : channels + 128] = lanes(peak, 128)
        out[:, channels + 128 :] = lanes(total, 128)


def fold(states, own, twin, gain, blocks):
    length, channels = own.shape
    shape = ((length, channels + 256), F32)
    first = states is None
    args = (gain, own, twin, *blocks, *(() if first else states))
    kernel = functools.partial(fold_kernel, len(blocks), first)
    return call(kernel, [shape, shape], args, 24 << 20)


def spread(column, width):
    return jnp.concatenate([column] * -(-width // 128), axis=1)[:, :width]


def combine_kernel(wv_ref, wo_ref, out_ref):
    out_ref[...] = dot(wv_ref[...], wo_ref[...]).astype(BF16)


def finish_kernel(
    height, state_ref, other_ref, query_ref, last_a_ref, last_b_ref, key_gain_ref, raw_ref, partial_ref,
    wvo_ref, gain_ref, bias_ref, w_ref, hidden_ref, mixed_ref,
):
    length, channels = raw_ref.shape
    count, out = partial_ref.shape
    slots = edge_slots(count // height)
    row = lax.axis_index("rows")
    col = lax.axis_index("cols")
    has_top, has_bottom = row > 0, row < lax.axis_size("rows") - 1
    has_left, has_right = col > 0, col < lax.axis_size("cols") - 1

    keys = key_rows((last_a_ref, last_b_ref), key_gain_ref[...])
    scores = dot_t(query_ref[...], keys)
    peak_a, total_a = state_ref[:, channels : channels + 128], state_ref[:, channels + 128 :]
    peak_b, total_b = other_ref[:, channels : channels + 128], other_ref[:, channels + 128 :]
    peak = jnp.maximum(peak_a, peak_b)
    peak = jnp.maximum(peak, lanes(jnp.max(scores, axis=1, keepdims=True), 128))
    fade_a, fade_b = jnp.exp(peak_a - peak), jnp.exp(peak_b - peak)
    weights = jnp.exp(scores - spread(peak, scores.shape[1]))
    total = lanes(jnp.sum(weights, axis=1, keepdims=True), 128)
    total = total + fade_a * total_a + fade_b * total_b
    summed = dot(weights.astype(BF16), keys)
    summed = summed + spread(fade_a, channels) * state_ref[:, :channels]
    summed = summed + spread(fade_b, channels) * other_ref[:, :channels]
    pooled = (summed * spread(1.0 / total, channels)).astype(BF16)
    hidden = (raw_ref[...].astype(F32) + dot(pooled, wvo_ref[...])).astype(BF16)
    wide = hidden.astype(F32)
    value = rms_scaled(wide, gain_ref[...])
    value = value / (1.0 + jnp.exp(-value))
    slot = lax.broadcasted_iota(jnp.int32, (length, 1), 0)
    main_end = length - slots
    width = count // height
    in_top, in_bottom = slot < slots, slot >= main_end
    in_left = (slot >= slots) & (slot < slots + height)
    in_right = (slot >= main_end - height) & (slot < main_end)
    in_left = in_left | (slot == slots - 1) | (slot == length - 1)
    in_right = in_right | (slot == width) | (slot == main_end + width)
    outside = (in_top & jnp.logical_not(has_top)) | (in_bottom & jnp.logical_not(has_bottom))
    outside = outside | (in_left & jnp.logical_not(has_left)) | (in_right & jnp.logical_not(has_right))
    rows = tap_rows(jnp.where(outside, 0.0, value), height, count)

    own = hidden[slots + height : slots + height + count]
    hidden_ref[...] = own
    result = partial_ref[...] + own[:, :out].astype(F32) + bias_ref[...]
    for i in range(3):
        taps = w_ref[2, i].reshape(-1, out)
        result = result + shifted_rows(dot(rows[i], taps), i, height, count)
    mixed_ref[...] = result.astype(BF16)


def narrow(cols):
    return cols == 4


def moved(value, pairs):
    return lax.ppermute(value, AXES, pairs)


def block(
    frame_in, norm_gain, w_query, w_key, w_value, w_out, conv_gain, conv_cache, w_conv, conv_bias
):
    height, width, channels = frame_in.shape
    out_channels = w_conv.shape[4]
    count = height * width
    chips, ring, twin_pairs, down, up, cross_pairs = permutations(
        lax.axis_size("rows"), lax.axis_size("cols")
    )
    frame_far = jnp.transpose(frame_in, (1, 0, 2))
    cache_far = jnp.transpose(conv_cache, (0, 2, 1, 3))
    gain_far = norm_gain.reshape(1, channels)

    rows = edge_rows(width)
    tiles = [(frame_far.shape, BF16), (cache_far.shape, BF16), (gain_far.shape, F32)]
    far_tiles = (frame_far, cache_far, gain_far)
    edge = ((3, rows, channels), BF16)
    side = ((3, side_slots(height), channels), BF16)
    keys = ((count, channels), BF16)
    sems = [pltpu.SemaphoreType.DMA((3,))]
    hops = (chips - 1) // 2
    if narrow(lax.axis_size("cols")):
        with_row = ((count + 2 * rows, channels), BF16)
        frame, cache, gain, chain_a, to_partner = call(
            pack_chain_kernel, tiles + [with_row, with_row], (), far_args=far_tiles, scratch=sems
        )
        partner = moved(to_partner, twin_pairs)
        arrived_a = moved(chain_a, ring)
        arrived_b = moved(partner, ring)
        (chain_a,) = call(cut_kernel, [keys], (arrived_a,))
        (chain_b,) = call(cut_kernel, [keys], (arrived_b,))
        (mine,) = call(split_kernel, [((6 * rows + 2 * height, channels), BF16)], (cache, arrived_a, arrived_b))
        theirs = moved(mine, twin_pairs)
        top, bottom, twin, to_cross = call(
            sort_edges_kernel, [edge, edge, side, side], (frame, cache, partner, mine, theirs)
        )
    else:
        frame, cache, gain, first_rows, last_rows = call(
            pack_rows_kernel, tiles + [edge, edge], (), far_args=far_tiles, scratch=sems
        )
        chain_a = frame_far.reshape(count, channels)
        chain_b = moved(chain_a, twin_pairs)
        chain_a = moved(chain_a, ring)
        chain_b = moved(chain_b, ring)
        top = moved(last_rows, down)
        bottom = moved(first_rows, up)
        to_twin, to_cross = call(pack_cols_kernel, [side, side], (frame, cache, top, bottom))
        twin = moved(to_twin, twin_pairs)
    cross = moved(to_cross, cross_pairs)
    blocks = [frame, chain_a, chain_b]
    for _ in range(1, hops):
        chain_a = moved(chain_a, ring)
        chain_b = moved(chain_b, ring)
        blocks += [chain_a, chain_b]
    last_a = moved(chain_a, ring)
    last_b = moved(last_a, twin_pairs)

    far_args = (
        w_query, w_key, w_value, w_out, conv_gain.reshape(1, channels),
        conv_bias.reshape(1, out_channels), w_conv,
    )
    w_query, w_key, w_value, w_out, conv_gain, conv_bias, w_conv = far_args
    (w_both,) = call(combine_kernel, [((channels, channels), BF16)], (w_value, w_out))
    ext = ((2 * edge_slots(width) + (width + 2) * height, channels), BF16)
    raw, queries = call(query_kernel, [ext, ext], (frame, top, bottom, twin, cross, gain, w_query, w_key))
    twin_queries = moved(queries, twin_pairs)
    (partial,) = call(cache_conv_kernel, [((count, out_channels), F32)], (cache, top, bottom, twin, cross, w_conv))
    states = None
    for k in range(0, len(blocks), 7):
        states = fold(states, queries, twin_queries, gain, blocks[k : k + 7])
    other = moved(states[1], twin_pairs)
    hidden, mixed = call(
        functools.partial(finish_kernel, height),
        [((count, channels), BF16), ((count, out_channels), BF16)],
        (
            states[0], other, queries, last_a, last_b, gain, raw, partial, w_both, conv_gain, conv_bias, w_conv,
        ),
        24 << 20,
        far=True,
    )
    hidden = jnp.transpose(hidden.reshape(width, height, channels), (1, 0, 2))
    mixed = jnp.transpose(mixed.reshape(width, height, out_channels), (1, 0, 2))
    return (hidden, mixed)


def solution(mesh):
    in_specs = (
        P(("video", "rows"), "cols", None),
        P(),
        P(),
        P(),
        P(),
        P(),
        P(),
        P(None, ("video", "rows"), "cols", None),
        P(),
        P(),
    )
    out_specs = (P(("video", "rows"), "cols", None), P(("video", "rows"), "cols", None))
    return jax.shard_map(block, mesh=mesh, in_specs=in_specs, out_specs=out_specs, check_vma=False)
```

```python
import functools
import math

import jax
import jax.numpy as jnp
from jax import lax
from jax.experimental import pallas as pl
from jax.experimental.pallas import tpu as pltpu
from jax.sharding import PartitionSpec as P


EPS = 1e-06
AXES = ("rows", "cols")
F32 = jnp.float32
COST = 2_000_000_000
BF16 = jnp.bfloat16
VM = pl.BlockSpec(memory_space=pltpu.VMEM)


def near(value):
    return pltpu.with_memory_space_constraint(value, pltpu.VMEM)


def call(kernel, outs, args, limit=16 << 20, far_args=(), far=False, scratch=()):
    return pl.pallas_call(
        kernel,
        in_specs=[VM] * len(args) + [pl.BlockSpec(memory_space=pltpu.HBM)] * len(far_args),
        out_specs=[VM] * len(outs),
        out_shape=[
            jax.ShapeDtypeStruct(shape, dtype) if far else pltpu.VMEM(shape, dtype)
            for shape, dtype in outs
        ],
        scratch_shapes=scratch,
        compiler_params=pltpu.CompilerParams(vmem_limit_bytes=limit),
        cost_estimate=pl.CostEstimate(flops=COST, bytes_accessed=4 << 20, transcendentals=0),
    )(*[near(a) for a in args], *[pltpu.with_memory_space_constraint(a, pltpu.HBM) for a in far_args])


def chip_cycle(height, width):
    if width == 1 or height == 1:
        return [(z, x) for z in range(height) for x in range(width)]
    order = []
    for x in range(width):
        inner = range(1, height) if x % 2 == 0 else range(height - 1, 0, -1)
        order += [(z, x) for z in inner]
    return order + [(0, x) for x in range(width - 1, -1, -1)]


def permutations(rows, cols):
    def at(z, x, core):
        return z * cols + 2 * x + core

    walk = chip_cycle(rows, cols // 2)
    ring = []
    for k, here in enumerate(walk):
        there = walk[(k + 1) % len(walk)]
        ring += [(at(*here, 0), at(*there, 0)), (at(*there, 1), at(*here, 1))]
    twin = [(i, i ^ 1) for i in range(rows * cols)]
    down = [(i, i + cols) for i in range((rows - 1) * cols)]
    up = [(j, i) for i, j in down]
    cross = []
    for r in range(rows):
        for c in range(1, cols - 1, 2):
            i = r * cols + c
            cross += [(i, i + 1), (i + 1, i)]
    return len(walk), ring, twin, down, up, cross


def edge_slots(width):
    return -(-(width + 2) // 8) * 8


def edge_rows(width):
    return -(-width // 8) * 8


def side_slots(height):
    return height + 8


def rms_scaled(values, gain):
    mean_sq = jnp.mean(values * values, axis=-1, keepdims=True)
    return values * lax.rsqrt(mean_sq + EPS) * gain


def dot(a, b):
    return jnp.dot(a, b, preferred_element_type=F32)


def dot_t(a, b):
    return lax.dot_general(a, b, (((1,), (1,)), ((), ())), preferred_element_type=F32)


def row_edge(tile, r):
    width, _, channels = tile.shape
    fill = jnp.zeros((edge_rows(width) - width, channels), F32)
    return jnp.concatenate([tile[c, r : r + 1, :] for c in range(width)] + [fill], axis=0)


def load_tiles(frame_hbm, cache_hbm, gain_hbm, frame_ref, cache_ref, gain_ref, sems):
    copies = [
        pltpu.make_async_copy(frame_hbm, frame_ref, sems.at[0]),
        pltpu.make_async_copy(cache_hbm, cache_ref, sems.at[1]),
        pltpu.make_async_copy(gain_hbm, gain_ref, sems.at[2]),
    ]
    for copy in copies:
        copy.start()
    for copy in copies:
        copy.wait()


def pack_rows_kernel(frame_hbm, cache_hbm, gain_hbm, frame_ref, cache_ref, gain_ref, first_ref, last_ref, sems):
    load_tiles(frame_hbm, cache_hbm, gain_hbm, frame_ref, cache_ref, gain_ref, sems)
    height = frame_ref.shape[1]
    for t in range(3):
        tile = (frame_ref[...] if t == 2 else cache_ref[t]).astype(F32)
        first_ref[t] = row_edge(tile, 0).astype(BF16)
        last_ref[t] = row_edge(tile, height - 1).astype(BF16)


def faces_up():
    col = lax.axis_index("cols")
    return lax.rem(lax.rem(col, 2) + lax.div(col, 2), 2)


def pack_chain_kernel(frame_hbm, cache_hbm, gain_hbm, frame_ref, cache_ref, gain_ref, chain_ref, swap_ref, sems):
    load_tiles(frame_hbm, cache_hbm, gain_hbm, frame_ref, cache_ref, gain_ref, sems)
    width, height, channels = frame_ref.shape
    count, rows = width * height, edge_rows(width)
    up = faces_up()
    chain_ref[:count] = frame_ref[...].reshape(count, channels)
    swap_ref[:count] = frame_ref[...].reshape(count, channels)
    for t in range(2):
        tile = cache_ref[t].astype(F32)
        first, last = row_edge(tile, 0), row_edge(tile, height - 1)
        at = count + t * rows
        chain_ref[at : at + rows] = jnp.where(up == 1, first, last).astype(BF16)
        swap_ref[at : at + rows] = jnp.where(up == 1, last, first).astype(BF16)


def cut_kernel(arrived_ref, chain_ref):
    chain_ref[...] = arrived_ref[: chain_ref.shape[0]]


def split_kernel(cache_ref, a_ref, b_ref, edges_ref):
    _, width, height, _ = cache_ref.shape
    count, rows = width * height, edge_rows(width)
    up = faces_up()
    odd = lax.rem(lax.axis_index("cols"), 2)
    for k, ref in enumerate((a_ref, b_ref)):
        to = k * 3 * rows
        edges_ref[to : to + 2 * rows] = ref[count : count + 2 * rows]
        tile = ref[:count].astype(F32).reshape(width, height, -1)
        edge = jnp.where(up == 1, row_edge(tile, 0), row_edge(tile, height - 1))
        edges_ref[to + 2 * rows : to + 3 * rows] = edge.astype(BF16)
    for t in range(2):
        at = 6 * rows + t * height
        column = jnp.where(odd == 1, cache_ref[t, 0].astype(F32), cache_ref[t, width - 1].astype(F32))
        edges_ref[at : at + height] = column.astype(BF16)


def sort_edges_kernel(
    frame_ref, cache_ref, partner_ref, mine_ref, theirs_ref, top_ref, bottom_ref, twin_ref, cross_ref
):
    width, height, channels = frame_ref.shape
    count, rows = width * height, top_ref.shape[1]
    up = faces_up()
    odd = lax.rem(lax.axis_index("cols"), 2)
    row = lax.axis_index("rows")
    has_top, has_bottom = row > 0, row < lax.axis_size("rows") - 1
    fill = jnp.zeros((side_slots(height) - height - 2, channels), F32)
    for t in range(3):
        pair = []
        for k in range(2):
            mine = mine_ref[(3 * k + t) * rows : (3 * k + t + 1) * rows].astype(F32)
            theirs = theirs_ref[(3 - 3 * k + t) * rows : (4 - 3 * k + t) * rows].astype(F32)
            top = jnp.where(has_top, jnp.where(up == 1, theirs, mine), 0.0)
            bottom = jnp.where(has_bottom, jnp.where(up == 1, mine, theirs), 0.0)
            pair.append((top, bottom))
        (top, bottom), (twin_top, twin_bottom) = pair
        top_ref[t] = top.astype(BF16)
        bottom_ref[t] = bottom.astype(BF16)

        def facing(first, value, axis_rows):
            a, b = value[axis_rows(0)], value[axis_rows(width - 1)]
            return jnp.where(first, a, b)

        if t == 2:
            block = partner_ref[:count].astype(F32)
            column = facing(odd == 0, block, lambda c: slice(c * height, (c + 1) * height))
        else:
            at = 6 * rows + t * height
            column = theirs_ref[at : at + height].astype(F32)
        corners = [facing(odd == 0, v, lambda c: slice(c, c + 1)) for v in (twin_top, twin_bottom)]
        twin_ref[t] = jnp.concatenate([column, *corners, fill], axis=0).astype(BF16)
        tile = (frame_ref[...] if t == 2 else cache_ref[t]).astype(F32)
        column = jnp.where(odd == 0, tile[0], tile[width - 1])
        corners = [facing(odd == 0, v, lambda c: slice(c, c + 1)) for v in (top, bottom)]
        cross_ref[t] = jnp.concatenate([column, *corners, fill], axis=0).astype(BF16)


def pack_cols_kernel(frame_ref, cache_ref, top_ref, bottom_ref, twin_ref, cross_ref):
    width, height, channels = frame_ref.shape
    odd = lax.rem(lax.axis_index("cols"), 2)
    fill = jnp.zeros((side_slots(height) - height - 2, channels), F32)
    for t in range(3):
        sides = []
        for c in (0, width - 1):
            own = (frame_ref[c] if t == 2 else cache_ref[t, c]).astype(F32)
            top = top_ref[t].astype(F32)[c : c + 1, :]
            bottom = bottom_ref[t].astype(F32)[c : c + 1, :]
            sides.append(jnp.concatenate([own, top, bottom, fill], axis=0))
        left, right = sides
        twin_ref[t] = jnp.where(odd == 1, left, right).astype(BF16)
        cross_ref[t] = jnp.where(odd == 1, right, left).astype(BF16)


def extended(own, top, bottom, twin, cross, odd):
    height = twin.shape[0] - side_slots(0)
    left = jnp.where(odd == 1, twin, cross)
    right = jnp.where(odd == 1, cross, twin)
    width = own.shape[0] // height
    slots = edge_slots(width)
    slot = lax.broadcasted_iota(jnp.int32, (slots, own.shape[1]), 0)
    spare = slots - top.shape[0]

    def edge(row, k):
        if spare:
            row = jnp.concatenate([row, jnp.zeros((spare, own.shape[1]), F32)], axis=0)
        row = jnp.where(slot == width, right[k : k + 1, :], row)
        return jnp.where(slot == slots - 1, left[k : k + 1, :], row)

    return jnp.concatenate(
        [edge(top, height), left[:height], own, right[:height], edge(bottom, height + 1)], axis=0
    )


def tap_rows(tokens, height, count):
    slots = edge_slots(count // height)
    main = tokens[slots : tokens.shape[0] - slots]
    mains = [main[j * height : j * height + count] for j in range(3)]
    result = []
    for edge in (tokens[:slots], None, tokens[tokens.shape[0] - slots :]):
        if edge is None:
            parts = mains
        else:
            edges = [pltpu.roll(edge, 1, 0), edge, pltpu.roll(edge, slots - 1, 0)]
            parts = [jnp.concatenate(pair, axis=0) for pair in zip(mains, edges)]
        result.append(jnp.concatenate([p.astype(BF16) for p in parts], axis=1))
    return result


def shifted_rows(sums, i, height, count):
    if i == 1:
        return sums
    main, edge = sums[:count], sums[count:]
    out = main.shape[1]
    width = count // height
    tile = main.reshape(width, height, out)
    moved = pltpu.roll(tile, 1 if i == 0 else height - 1, 1)
    row = lax.broadcasted_iota(jnp.int32, (height, out), 0)
    at = 0 if i == 0 else height - 1
    cells = [jnp.where(row == at, edge[c : c + 1, :], moved[c]) for c in range(width)]
    return jnp.concatenate(cells, axis=0)


def cache_conv_kernel(cache_ref, top_ref, bottom_ref, twin_ref, cross_ref, w_ref, out_ref):
    width, height, channels = cache_ref.shape[1:]
    count = width * height
    odd = lax.rem(lax.axis_index("cols"), 2)
    rows = [
        tap_rows(
            extended(
                cache_ref[t].reshape(count, channels).astype(F32),
                top_ref[t].astype(F32),
                bottom_ref[t].astype(F32),
                twin_ref[t].astype(F32),
                cross_ref[t].astype(F32),
                odd,
            ),
            height,
            count,
        )
        for t in range(2)
    ]
    result = None
    for i in range(3):
        patches = jnp.concatenate([rows[0][i], rows[1][i]], axis=1)
        taps = w_ref[:2, i].reshape(-1, w_ref.shape[4])
        value = shifted_rows(dot(patches, taps), i, height, count)
        result = value if result is None else result + value
    out_ref[...] = result


def query_kernel(
    frame_ref, top_ref, bottom_ref, twin_ref, cross_ref, gain_ref, wqk_ref, raw_ref, keys_ref
):
    width, height, channels = frame_ref.shape
    odd = lax.rem(lax.axis_index("cols"), 2)
    tokens = extended(
        frame_ref[...].reshape(width * height, channels).astype(F32),
        top_ref[2].astype(F32),
        bottom_ref[2].astype(F32),
        twin_ref[2].astype(F32),
        cross_ref[2].astype(F32),
        odd,
    )
    raw_ref[...] = tokens.astype(BF16)
    normed = rms_scaled(tokens, gain_ref[...]).astype(BF16)
    keys_ref[...] = (dot(normed, wqk_ref[...]) * (1.0 / math.sqrt(channels))).astype(BF16)


def lanes(value, width):
    return jnp.broadcast_to(value, (value.shape[0], width))


def key_rows(refs, gain):
    parts = [
        rms_scaled(ref[...].reshape(-1, gain.shape[1]).astype(F32), gain).astype(BF16) for ref in refs
    ]
    return parts[0] if len(parts) == 1 else jnp.concatenate(parts, axis=0)


def fold_kernel(blocks, first, last, gain_ref, own_ref, twin_ref, *refs):
    keys = key_rows(refs[:blocks], gain_ref[...])
    refs = refs[blocks:]
    states, outs = ((None, None), refs) if first else (refs[:2], refs[2:])
    channels = keys.shape[1]
    length = own_ref.shape[0]
    all_scores = dot_t(jnp.concatenate([own_ref[...], twin_ref[...]], axis=0), keys)
    peaks, totals, weights = [], [], []
    for k, state in enumerate(states):
        scores = all_scores[k * length : (k + 1) * length]
        peak = jnp.max(scores, axis=1, keepdims=True)
        if not first:
            peak = jnp.maximum(peak, state[:, channels : channels + 1])
        part = jnp.exp(scores - peak)
        peaks.append(peak)
        totals.append(jnp.sum(part, axis=1, keepdims=True))
        weights.append(part.astype(BF16))
    all_summed = dot(jnp.concatenate(weights, axis=0), keys)
    for k, (state, out) in enumerate(zip(states, outs)):
        summed, total, peak = all_summed[k * length : (k + 1) * length], totals[k], peaks[k]
        if not first:
            fade = jnp.exp(state[:, channels : channels + 1] - peak)
            total = total + fade * state[:, channels + 128 : channels + 129]
            summed = summed + fade * state[:, :channels]
        if last and k == 1:
            out[...] = summed.astype(BF16)
            outs[2][:, :128] = lanes(peak, 128)
            outs[2][:, 128:] = lanes(total, 128)
        else:
            out[:, :channels] = summed
            out[:, channels : channels + 128] = lanes(peak, 128)
            out[:, channels + 128 :] = lanes(total, 128)


def fold(states, own, twin, gain, blocks, last):
    length, channels = own.shape
    shape = ((length, channels + 256), F32)
    first = states is None
    args = (gain, own, twin, *blocks, *(() if first else states))
    kernel = functools.partial(fold_kernel, len(blocks), first, last)
    others = [((length, channels), BF16), ((length, 256), F32)] if last else [shape]
    return call(kernel, [shape, *others], args, 24 << 20)


def spread(column, width):
    return jnp.concatenate([column] * -(-width // 128), axis=1)[:, :width]


def fold_own_kernel(gain_ref, query_ref, block_ref, state_ref, out_ref):
    keys = key_rows((block_ref,), gain_ref[...])
    channels = keys.shape[1]
    scores = dot_t(query_ref[...], keys)
    before = state_ref[:, channels : channels + 128]
    peak = jnp.maximum(before, lanes(jnp.max(scores, axis=1, keepdims=True), 128))
    fade = jnp.exp(before - peak)
    weights = jnp.exp(scores - spread(peak, scores.shape[1]))
    total = lanes(jnp.sum(weights, axis=1, keepdims=True), 128)
    summed = dot(weights.astype(BF16), keys)
    out_ref[:, :channels] = summed + spread(fade, channels) * state_ref[:, :channels]
    out_ref[:, channels : channels + 128] = peak
    out_ref[:, channels + 128 :] = total + fade * state_ref[:, channels + 128 :]


def combine_kernel(wq_ref, wk_ref, wv_ref, wo_ref, query_key_ref, value_out_ref):
    query_key_ref[...] = dot_t(wq_ref[...], wk_ref[...]).astype(BF16)
    value_out_ref[...] = dot(wv_ref[...], wo_ref[...]).astype(BF16)


def finish_kernel(
    height, state_ref, other_ref, scale_ref, query_ref, last_ref, key_gain_ref, raw_ref, partial_ref,
    wvo_ref, gain_ref, bias_ref, w_ref, hidden_ref, mixed_ref,
):
    length, channels = raw_ref.shape
    count, out = partial_ref.shape
    slots = edge_slots(count // height)
    row = lax.axis_index("rows")
    col = lax.axis_index("cols")
    has_top, has_bottom = row > 0, row < lax.axis_size("rows") - 1
    has_left, has_right = col > 0, col < lax.axis_size("cols") - 1

    keys = key_rows((last_ref,), key_gain_ref[...])
    scores = dot_t(query_ref[...], keys)
    peak_a, total_a = state_ref[:, channels : channels + 128], state_ref[:, channels + 128 :]
    peak_b, total_b = scale_ref[:, :128], scale_ref[:, 128:]
    peak = jnp.maximum(peak_a, peak_b)
    peak = jnp.maximum(peak, lanes(jnp.max(scores, axis=1, keepdims=True), 128))
    fade_a, fade_b = jnp.exp(peak_a - peak), jnp.exp(peak_b - peak)
    weights = jnp.exp(scores - spread(peak, scores.shape[1]))
    total = lanes(jnp.sum(weights, axis=1, keepdims=True), 128)
    total = total + fade_a * total_a + fade_b * total_b
    summed = dot(weights.astype(BF16), keys)
    summed = summed + spread(fade_a, channels) * state_ref[:, :channels]
    summed = summed + spread(fade_b, channels) * other_ref[...].astype(F32)
    pooled = (summed * spread(1.0 / total, channels)).astype(BF16)
    hidden = (raw_ref[...].astype(F32) + dot(pooled, wvo_ref[...])).astype(BF16)
    wide = hidden.astype(F32)
    value = rms_scaled(wide, gain_ref[...])
    value = value / (1.0 + jnp.exp(-value))
    slot = lax.broadcasted_iota(jnp.int32, (length, 1), 0)
    main_end = length - slots
    width = count // height
    in_top, in_bottom = slot < slots, slot >= main_end
    in_left = (slot >= slots) & (slot < slots + height)
    in_right = (slot >= main_end - height) & (slot < main_end)
    in_left = in_left | (slot == slots - 1) | (slot == length - 1)
    in_right = in_right | (slot == width) | (slot == main_end + width)
    outside = (in_top & jnp.logical_not(has_top)) | (in_bottom & jnp.logical_not(has_bottom))
    outside = outside | (in_left & jnp.logical_not(has_left)) | (in_right & jnp.logical_not(has_right))
    rows = tap_rows(jnp.where(outside, 0.0, value), height, count)

    own = hidden[slots + height : slots + height + count]
    hidden_ref[...] = own
    result = partial_ref[...] + own[:, :out].astype(F32) + bias_ref[...]
    for i in range(3):
        taps = w_ref[2, i].reshape(-1, out)
        result = result + shifted_rows(dot(rows[i], taps), i, height, count)
    mixed_ref[...] = result.astype(BF16)


def narrow(cols):
    return cols == 4


def moved(value, pairs):
    return lax.ppermute(value, AXES, pairs)


def block(
    frame_in, norm_gain, w_query, w_key, w_value, w_out, conv_gain, conv_cache, w_conv, conv_bias
):
    height, width, channels = frame_in.shape
    out_channels = w_conv.shape[4]
    count = height * width
    chips, ring, twin_pairs, down, up, cross_pairs = permutations(
        lax.axis_size("rows"), lax.axis_size("cols")
    )
    frame_far = jnp.transpose(frame_in, (1, 0, 2))
    cache_far = jnp.transpose(conv_cache, (0, 2, 1, 3))
    gain_far = norm_gain.reshape(1, channels)

    rows = edge_rows(width)
    tiles = [(frame_far.shape, BF16), (cache_far.shape, BF16), (gain_far.shape, F32)]
    far_tiles = (frame_far, cache_far, gain_far)
    edge = ((3, rows, channels), BF16)
    side = ((3, side_slots(height), channels), BF16)
    keys = ((count, channels), BF16)
    sems = [pltpu.SemaphoreType.DMA((3,))]
    hops = (chips - 1) // 2
    if narrow(lax.axis_size("cols")):
        with_row = ((count + 2 * rows, channels), BF16)
        frame, cache, gain, chain_a, to_partner = call(
            pack_chain_kernel, tiles + [with_row, with_row], (), far_args=far_tiles, scratch=sems
        )
        partner = moved(to_partner, twin_pairs)
        arrived_a = moved(chain_a, ring)
        arrived_b = moved(partner, ring)
        (chain_a,) = call(cut_kernel, [keys], (arrived_a,))
        (chain_b,) = call(cut_kernel, [keys], (arrived_b,))
        (mine,) = call(split_kernel, [((6 * rows + 2 * height, channels), BF16)], (cache, arrived_a, arrived_b))
        theirs = moved(mine, twin_pairs)
        top, bottom, twin, to_cross = call(
            sort_edges_kernel, [edge, edge, side, side], (frame, cache, partner, mine, theirs)
        )
    else:
        frame, cache, gain, first_rows, last_rows = call(
            pack_rows_kernel, tiles + [edge, edge], (), far_args=far_tiles, scratch=sems
        )
        chain_a = frame_far.reshape(count, channels)
        chain_b = moved(chain_a, twin_pairs)
        chain_a = moved(chain_a, ring)
        chain_b = moved(chain_b, ring)
        top = moved(last_rows, down)
        bottom = moved(first_rows, up)
        to_twin, to_cross = call(pack_cols_kernel, [side, side], (frame, cache, top, bottom))
        twin = moved(to_twin, twin_pairs)
    cross = moved(to_cross, cross_pairs)
    blocks = [frame, chain_a, chain_b]
    for _ in range(1, hops):
        chain_a = moved(chain_a, ring)
        chain_b = moved(chain_b, ring)
        blocks += [chain_a, chain_b]
    last_a = moved(chain_a, ring)
    last_b = moved(last_a, twin_pairs)

    far_args = (
        w_query, w_key, w_value, w_out, conv_gain.reshape(1, channels),
        conv_bias.reshape(1, out_channels), w_conv,
    )
    w_query, w_key, w_value, w_out, conv_gain, conv_bias, w_conv = far_args
    square = ((channels, channels), BF16)
    w_query_key, w_value_out = call(combine_kernel, [square, square], (w_query, w_key, w_value, w_out))
    ext = ((2 * edge_slots(width) + (width + 2) * height, channels), BF16)
    raw, queries = call(query_kernel, [ext, ext], (frame, top, bottom, twin, cross, gain, w_query_key))
    twin_queries = moved(queries, twin_pairs)
    (partial,) = call(cache_conv_kernel, [((count, out_channels), F32)], (cache, top, bottom, twin, cross, w_conv))
    states = None
    for k in range(0, len(blocks), 7):
        states = fold(states, queries, twin_queries, gain, blocks[k : k + 7], k + 7 >= len(blocks))
    other = moved(states[1], twin_pairs)
    other_scale = moved(states[2], twin_pairs)
    (state,) = call(fold_own_kernel, [(states[0].shape, F32)], (gain, queries, last_a, states[0]))
    hidden, mixed = call(
        functools.partial(finish_kernel, height),
        [((count, channels), BF16), ((count, out_channels), BF16)],
        (
            state, other, other_scale, queries, last_b, gain, raw, partial, w_value_out, conv_gain, conv_bias, w_conv,
        ),
        24 << 20,
        far=True,
    )
    hidden = jnp.transpose(hidden.reshape(width, height, channels), (1, 0, 2))
    mixed = jnp.transpose(mixed.reshape(width, height, out_channels), (1, 0, 2))
    return (hidden, mixed)


def solution(mesh):
    in_specs = (
        P(("video", "rows"), "cols", None),
        P(),
        P(),
        P(),
        P(),
        P(),
        P(),
        P(None, ("video", "rows"), "cols", None),
        P(),
        P(),
    )
    out_specs = (P(("video", "rows"), "cols", None), P(("video", "rows"), "cols", None))
    return jax.shard_map(block, mesh=mesh, in_specs=in_specs, out_specs=out_specs, check_vma=False)
```

```python
import functools
import math

import jax
import jax.numpy as jnp
from jax import lax
from jax.experimental import pallas as pl
from jax.experimental.pallas import tpu as pltpu
from jax.sharding import PartitionSpec as P


EPS = 1e-06
AXES = ("rows", "cols")
F32 = jnp.float32
COST = 2_000_000_000
BF16 = jnp.bfloat16
VM = pl.BlockSpec(memory_space=pltpu.VMEM)


def near(value):
    return pltpu.with_memory_space_constraint(value, pltpu.VMEM)


def call(kernel, outs, args, limit=16 << 20, far_args=(), far=False, scratch=()):
    return pl.pallas_call(
        kernel,
        in_specs=[VM] * len(args) + [pl.BlockSpec(memory_space=pltpu.HBM)] * len(far_args),
        out_specs=[VM] * len(outs),
        out_shape=[
            jax.ShapeDtypeStruct(shape, dtype) if far else pltpu.VMEM(shape, dtype)
            for shape, dtype in outs
        ],
        scratch_shapes=scratch,
        compiler_params=pltpu.CompilerParams(vmem_limit_bytes=limit),
        cost_estimate=pl.CostEstimate(flops=COST, bytes_accessed=4 << 20, transcendentals=0),
    )(*[near(a) for a in args], *[pltpu.with_memory_space_constraint(a, pltpu.HBM) for a in far_args])


def chip_cycle(height, width):
    if width == 1 or height == 1:
        return [(z, x) for z in range(height) for x in range(width)]
    order = []
    for x in range(width):
        inner = range(1, height) if x % 2 == 0 else range(height - 1, 0, -1)
        order += [(z, x) for z in inner]
    return order + [(0, x) for x in range(width - 1, -1, -1)]


def permutations(rows, cols):
    def at(z, x, core):
        return z * cols + 2 * x + core

    walk = chip_cycle(rows, cols // 2)
    ring = []
    for k, here in enumerate(walk):
        there = walk[(k + 1) % len(walk)]
        ring += [(at(*here, 0), at(*there, 0)), (at(*there, 1), at(*here, 1))]
    twin = [(i, i ^ 1) for i in range(rows * cols)]
    down = [(i, i + cols) for i in range((rows - 1) * cols)]
    up = [(j, i) for i, j in down]
    cross = []
    for r in range(rows):
        for c in range(1, cols - 1, 2):
            i = r * cols + c
            cross += [(i, i + 1), (i + 1, i)]
    return len(walk), ring, twin, down, up, cross


def edge_slots(width):
    return -(-(width + 2) // 8) * 8


def edge_rows(width):
    return -(-width // 8) * 8


def side_slots(height):
    return height + 8


def rms_scaled(values, gain):
    mean_sq = jnp.mean(values * values, axis=-1, keepdims=True)
    return values * lax.rsqrt(mean_sq + EPS) * gain


def dot(a, b):
    return jnp.dot(a, b, preferred_element_type=F32)


def dot_t(a, b):
    return lax.dot_general(a, b, (((1,), (1,)), ((), ())), preferred_element_type=F32)


def row_edge(tile, r):
    width, _, channels = tile.shape
    fill = jnp.zeros((edge_rows(width) - width, channels), F32)
    return jnp.concatenate([tile[c, r : r + 1, :] for c in range(width)] + [fill], axis=0)


def load_tiles(frame_hbm, cache_hbm, gain_hbm, frame_ref, cache_ref, gain_ref, sems):
    copies = [
        pltpu.make_async_copy(frame_hbm, frame_ref, sems.at[0]),
        pltpu.make_async_copy(cache_hbm, cache_ref, sems.at[1]),
        pltpu.make_async_copy(gain_hbm, gain_ref, sems.at[2]),
    ]
    for copy in copies:
        copy.start()
    for copy in copies:
        copy.wait()


def pack_rows_kernel(frame_hbm, cache_hbm, gain_hbm, frame_ref, cache_ref, gain_ref, first_ref, last_ref, sems):
    load_tiles(frame_hbm, cache_hbm, gain_hbm, frame_ref, cache_ref, gain_ref, sems)
    height = frame_ref.shape[1]
    for t in range(3):
        tile = (frame_ref[...] if t == 2 else cache_ref[t]).astype(F32)
        first_ref[t] = row_edge(tile, 0).astype(BF16)
        last_ref[t] = row_edge(tile, height - 1).astype(BF16)


def faces_up():
    col = lax.axis_index("cols")
    return lax.rem(lax.rem(col, 2) + lax.div(col, 2), 2)


def pack_chain_kernel(frame_hbm, cache_hbm, gain_hbm, frame_ref, cache_ref, gain_ref, chain_ref, swap_ref, sems):
    load_tiles(frame_hbm, cache_hbm, gain_hbm, frame_ref, cache_ref, gain_ref, sems)
    width, height, channels = frame_ref.shape
    count, rows = width * height, edge_rows(width)
    up = faces_up()
    chain_ref[:count] = frame_ref[...].reshape(count, channels)
    swap_ref[:count] = frame_ref[...].reshape(count, channels)
    for t in range(2):
        tile = cache_ref[t].astype(F32)
        first, last = row_edge(tile, 0), row_edge(tile, height - 1)
        at = count + t * rows
        chain_ref[at : at + rows] = jnp.where(up == 1, first, last).astype(BF16)
        swap_ref[at : at + rows] = jnp.where(up == 1, last, first).astype(BF16)


def cut_kernel(arrived_ref, chain_ref):
    chain_ref[...] = arrived_ref[: chain_ref.shape[0]]


def split_kernel(cache_ref, a_ref, b_ref, edges_ref):
    _, width, height, _ = cache_ref.shape
    count, rows = width * height, edge_rows(width)
    up = faces_up()
    odd = lax.rem(lax.axis_index("cols"), 2)
    for k, ref in enumerate((a_ref, b_ref)):
        to = k * 3 * rows
        edges_ref[to : to + 2 * rows] = ref[count : count + 2 * rows]
        tile = ref[:count].astype(F32).reshape(width, height, -1)
        edge = jnp.where(up == 1, row_edge(tile, 0), row_edge(tile, height - 1))
        edges_ref[to + 2 * rows : to + 3 * rows] = edge.astype(BF16)
    for t in range(2):
        at = 6 * rows + t * height
        column = jnp.where(odd == 1, cache_ref[t, 0].astype(F32), cache_ref[t, width - 1].astype(F32))
        edges_ref[at : at + height] = column.astype(BF16)


def sort_edges_kernel(
    frame_ref, cache_ref, partner_ref, mine_ref, theirs_ref, top_ref, bottom_ref, twin_ref, cross_ref
):
    width, height, channels = frame_ref.shape
    count, rows = width * height, top_ref.shape[1]
    up = faces_up()
    odd = lax.rem(lax.axis_index("cols"), 2)
    row = lax.axis_index("rows")
    has_top, has_bottom = row > 0, row < lax.axis_size("rows") - 1
    fill = jnp.zeros((side_slots(height) - height - 2, channels), F32)
    columns, ends = [], []
    for t in range(3):
        pair = []
        for k in range(2):
            mine = mine_ref[(3 * k + t) * rows : (3 * k + t + 1) * rows].astype(F32)
            theirs = theirs_ref[(3 - 3 * k + t) * rows : (4 - 3 * k + t) * rows].astype(F32)
            top = jnp.where(has_top, jnp.where(up == 1, theirs, mine), 0.0)
            bottom = jnp.where(has_bottom, jnp.where(up == 1, mine, theirs), 0.0)
            pair.append((top, bottom))
        (top, bottom), (twin_top, twin_bottom) = pair
        top_ref[t] = top.astype(BF16)
        bottom_ref[t] = bottom.astype(BF16)

        def facing(first, value, axis_rows):
            a, b = value[axis_rows(0)], value[axis_rows(width - 1)]
            return jnp.where(first, a, b)

        if t == 2:
            block = partner_ref[:count].astype(F32)
            column = facing(odd == 0, block, lambda c: slice(c * height, (c + 1) * height))
        else:
            at = 6 * rows + t * height
            column = theirs_ref[at : at + height].astype(F32)
        corners = [facing(odd == 0, v, lambda c: slice(c, c + 1)) for v in (twin_top, twin_bottom)]
        twin_ref[t] = jnp.concatenate([column, *corners, fill], axis=0).astype(BF16)
        tile = (frame_ref[...] if t == 2 else cache_ref[t]).astype(F32)
        column = jnp.where(odd == 0, tile[0], tile[width - 1])
        corners = [facing(odd == 0, v, lambda c: slice(c, c + 1)) for v in (top, bottom)]
        columns.append(column)
        ends += corners
    cross_ref[...] = to_side(columns, ends)


def pack_cols_kernel(frame_ref, cache_ref, top_ref, bottom_ref, twin_ref, cross_ref):
    width, height, channels = frame_ref.shape
    odd = lax.rem(lax.axis_index("cols"), 2)
    fill = jnp.zeros((side_slots(height) - height - 2, channels), F32)
    columns, ends = [], []
    for t in range(3):
        sides = []
        for c in (0, width - 1):
            own = (frame_ref[c] if t == 2 else cache_ref[t, c]).astype(F32)
            top = top_ref[t].astype(F32)[c : c + 1, :]
            bottom = bottom_ref[t].astype(F32)[c : c + 1, :]
            sides.append(jnp.concatenate([own, top, bottom, fill], axis=0))
        left, right = sides
        twin_ref[t] = jnp.where(odd == 1, left, right).astype(BF16)
        side = jnp.where(odd == 1, right, left)
        columns.append(side[:height])
        ends.append(side[height : height + 2])
    cross_ref[...] = to_side(columns, [e[k : k + 1] for e in ends for k in range(2)])


def extended(own, top, bottom, twin, cross, odd):
    height = twin.shape[0] - side_slots(0)
    left = jnp.where(odd == 1, twin, cross)
    right = jnp.where(odd == 1, cross, twin)
    width = own.shape[0] // height
    slots = edge_slots(width)
    slot = lax.broadcasted_iota(jnp.int32, (slots, own.shape[1]), 0)
    spare = slots - top.shape[0]

    def edge(row, k):
        if spare:
            row = jnp.concatenate([row, jnp.zeros((spare, own.shape[1]), F32)], axis=0)
        row = jnp.where(slot == width, right[k : k + 1, :], row)
        return jnp.where(slot == slots - 1, left[k : k + 1, :], row)

    return jnp.concatenate(
        [edge(top, height), left[:height], own, right[:height], edge(bottom, height + 1)], axis=0
    )


def from_side(ref, t):
    height = (ref.shape[0] - 8) // 3
    side = ref[...].astype(F32)
    fill = jnp.zeros((side_slots(height) - height - 2, side.shape[1]), F32)
    at = 3 * height + 2 * t
    return jnp.concatenate([side[t * height : (t + 1) * height], side[at : at + 2], fill], axis=0)


def to_side(columns, corners):
    fill = jnp.zeros((8 - len(corners), corners[0].shape[1]), F32)
    return jnp.concatenate([*columns, *corners, fill], axis=0).astype(BF16)


def tap_rows(tokens, height, count):
    slots = edge_slots(count // height)
    main = tokens[slots : tokens.shape[0] - slots]
    mains = [main[j * height : j * height + count] for j in range(3)]
    result = []
    for edge in (tokens[:slots], None, tokens[tokens.shape[0] - slots :]):
        if edge is None:
            parts = mains
        else:
            edges = [pltpu.roll(edge, 1, 0), edge, pltpu.roll(edge, slots - 1, 0)]
            parts = [jnp.concatenate(pair, axis=0) for pair in zip(mains, edges)]
        result.append(jnp.concatenate([p.astype(BF16) for p in parts], axis=1))
    return result


def shifted_rows(sums, i, height, count):
    if i == 1:
        return sums
    main, edge = sums[:count], sums[count:]
    out = main.shape[1]
    width = count // height
    tile = main.reshape(width, height, out)
    moved = pltpu.roll(tile, 1 if i == 0 else height - 1, 1)
    row = lax.broadcasted_iota(jnp.int32, (height, out), 0)
    at = 0 if i == 0 else height - 1
    cells = [jnp.where(row == at, edge[c : c + 1, :], moved[c]) for c in range(width)]
    return jnp.concatenate(cells, axis=0)


def cache_conv_kernel(cache_ref, top_ref, bottom_ref, twin_ref, cross_ref, w_ref, out_ref):
    width, height, channels = cache_ref.shape[1:]
    count = width * height
    odd = lax.rem(lax.axis_index("cols"), 2)
    rows = [
        tap_rows(
            extended(
                cache_ref[t].reshape(count, channels).astype(F32),
                top_ref[t].astype(F32),
                bottom_ref[t].astype(F32),
                twin_ref[t].astype(F32),
                from_side(cross_ref, t),
                odd,
            ),
            height,
            count,
        )
        for t in range(2)
    ]
    result = None
    for i in range(3):
        patches = jnp.concatenate([rows[0][i], rows[1][i]], axis=1)
        taps = w_ref[:2, i].reshape(-1, w_ref.shape[4])
        value = shifted_rows(dot(patches, taps), i, height, count)
        result = value if result is None else result + value
    out_ref[...] = result


def query_kernel(
    frame_ref, top_ref, bottom_ref, twin_ref, cross_ref, gain_ref, wqk_ref, raw_ref, keys_ref
):
    width, height, channels = frame_ref.shape
    odd = lax.rem(lax.axis_index("cols"), 2)
    tokens = extended(
        frame_ref[...].reshape(width * height, channels).astype(F32),
        top_ref[2].astype(F32),
        bottom_ref[2].astype(F32),
        twin_ref[2].astype(F32),
        from_side(cross_ref, 2),
        odd,
    )
    raw_ref[...] = tokens.astype(BF16)
    normed = rms_scaled(tokens, gain_ref[...]).astype(BF16)
    keys_ref[...] = (dot(normed, wqk_ref[...]) * (1.0 / math.sqrt(channels))).astype(BF16)


def lanes(value, width):
    return jnp.broadcast_to(value, (value.shape[0], width))


def key_rows(refs, gain):
    parts = [
        rms_scaled(ref[...].reshape(-1, gain.shape[1]).astype(F32), gain).astype(BF16) for ref in refs
    ]
    return parts[0] if len(parts) == 1 else jnp.concatenate(parts, axis=0)


def fold_kernel(blocks, first, last, gain_ref, own_ref, twin_ref, *refs):
    keys = key_rows(refs[:blocks], gain_ref[...])
    refs = refs[blocks:]
    states, outs = ((None, None), refs) if first else (refs[:2], refs[2:])
    channels = keys.shape[1]
    length = own_ref.shape[0]
    all_scores = dot_t(jnp.concatenate([own_ref[...], twin_ref[...]], axis=0), keys)
    peaks, totals, weights = [], [], []
    for k, state in enumerate(states):
        scores = all_scores[k * length : (k + 1) * length]
        peak = jnp.max(scores, axis=1, keepdims=True)
        if not first:
            peak = jnp.maximum(peak, state[:, channels : channels + 1])
        part = jnp.exp(scores - peak)
        peaks.append(peak)
        totals.append(jnp.sum(part, axis=1, keepdims=True))
        weights.append(part.astype(BF16))
    all_summed = dot(jnp.concatenate(weights, axis=0), keys)
    for k, (state, out) in enumerate(zip(states, outs)):
        summed, total, peak = all_summed[k * length : (k + 1) * length], totals[k], peaks[k]
        if not first:
            fade = jnp.exp(state[:, channels : channels + 1] - peak)
            total = total + fade * state[:, channels + 128 : channels + 129]
            summed = summed + fade * state[:, :channels]
        if last and k == 1:
            out[...] = summed.astype(BF16)
            outs[2][:, :128] = lanes(peak, 128)
            outs[2][:, 128:] = lanes(total, 128)
        else:
            out[:, :channels] = summed
            out[:, channels : channels + 128] = lanes(peak, 128)
            out[:, channels + 128 :] = lanes(total, 128)


def fold(states, own, twin, gain, blocks, last):
    length, channels = own.shape
    shape = ((length, channels + 256), F32)
    first = states is None
    args = (gain, own, twin, *blocks, *(() if first else states))
    kernel = functools.partial(fold_kernel, len(blocks), first, last)
    others = [((length, channels), BF16), ((length, 256), F32)] if last else [shape]
    return call(kernel, [shape, *others], args, 24 << 20)


def spread(column, width):
    return jnp.concatenate([column] * -(-width // 128), axis=1)[:, :width]


def fold_own_kernel(gain_ref, query_ref, block_ref, state_ref, out_ref):
    keys = key_rows((block_ref,), gain_ref[...])
    channels = keys.shape[1]
    scores = dot_t(query_ref[...], keys)
    before = state_ref[:, channels : channels + 128]
    peak = jnp.maximum(before, lanes(jnp.max(scores, axis=1, keepdims=True), 128))
    fade = jnp.exp(before - peak)
    weights = jnp.exp(scores - spread(peak, scores.shape[1]))
    total = lanes(jnp.sum(weights, axis=1, keepdims=True), 128)
    summed = dot(weights.astype(BF16), keys)
    out_ref[:, :channels] = summed + spread(fade, channels) * state_ref[:, :channels]
    out_ref[:, channels : channels + 128] = peak
    out_ref[:, channels + 128 :] = total + fade * state_ref[:, channels + 128 :]


def combine_kernel(wq_ref, wk_ref, wv_ref, wo_ref, query_key_ref, value_out_ref):
    query_key_ref[...] = dot_t(wq_ref[...], wk_ref[...]).astype(BF16)
    value_out_ref[...] = dot(wv_ref[...], wo_ref[...]).astype(BF16)


def finish_kernel(
    height, state_ref, other_ref, scale_ref, query_ref, last_ref, key_gain_ref, raw_ref, partial_ref,
    wvo_ref, gain_ref, bias_ref, w_ref, hidden_ref, mixed_ref,
):
    length, channels = raw_ref.shape
    count, out = partial_ref.shape
    slots = edge_slots(count // height)
    row = lax.axis_index("rows")
    col = lax.axis_index("cols")
    has_top, has_bottom = row > 0, row < lax.axis_size("rows") - 1
    has_left, has_right = col > 0, col < lax.axis_size("cols") - 1

    keys = key_rows((last_ref,), key_gain_ref[...])
    scores = dot_t(query_ref[...], keys)
    peak_a, total_a = state_ref[:, channels : channels + 128], state_ref[:, channels + 128 :]
    peak_b, total_b = scale_ref[:, :128], scale_ref[:, 128:]
    peak = jnp.maximum(peak_a, peak_b)
    peak = jnp.maximum(peak, lanes(jnp.max(scores, axis=1, keepdims=True), 128))
    fade_a, fade_b = jnp.exp(peak_a - peak), jnp.exp(peak_b - peak)
    weights = jnp.exp(scores - spread(peak, scores.shape[1]))
    total = lanes(jnp.sum(weights, axis=1, keepdims=True), 128)
    total = total + fade_a * total_a + fade_b * total_b
    summed = dot(weights.astype(BF16), keys)
    summed = summed + spread(fade_a, channels) * state_ref[:, :channels]
    summed = summed + spread(fade_b, channels) * other_ref[...].astype(F32)
    pooled = (summed * spread(1.0 / total, channels)).astype(BF16)
    hidden = (raw_ref[...].astype(F32) + dot(pooled, wvo_ref[...])).astype(BF16)
    wide = hidden.astype(F32)
    value = rms_scaled(wide, gain_ref[...])
    value = value / (1.0 + jnp.exp(-value))
    slot = lax.broadcasted_iota(jnp.int32, (length, 1), 0)
    main_end = length - slots
    width = count // height
    in_top, in_bottom = slot < slots, slot >= main_end
    in_left = (slot >= slots) & (slot < slots + height)
    in_right = (slot >= main_end - height) & (slot < main_end)
    in_left = in_left | (slot == slots - 1) | (slot == length - 1)
    in_right = in_right | (slot == width) | (slot == main_end + width)
    outside = (in_top & jnp.logical_not(has_top)) | (in_bottom & jnp.logical_not(has_bottom))
    outside = outside | (in_left & jnp.logical_not(has_left)) | (in_right & jnp.logical_not(has_right))
    rows = tap_rows(jnp.where(outside, 0.0, value), height, count)

    own = hidden[slots + height : slots + height + count]
    hidden_ref[...] = own
    result = partial_ref[...] + own[:, :out].astype(F32) + bias_ref[...]
    for i in range(3):
        taps = w_ref[2, i].reshape(-1, out)
        result = result + shifted_rows(dot(rows[i], taps), i, height, count)
    mixed_ref[...] = result.astype(BF16)


def narrow(cols):
    return cols == 4


def moved(value, pairs):
    return lax.ppermute(value, AXES, pairs)


def block(
    frame_in, norm_gain, w_query, w_key, w_value, w_out, conv_gain, conv_cache, w_conv, conv_bias
):
    height, width, channels = frame_in.shape
    out_channels = w_conv.shape[4]
    count = height * width
    chips, ring, twin_pairs, down, up, cross_pairs = permutations(
        lax.axis_size("rows"), lax.axis_size("cols")
    )
    frame_far = jnp.transpose(frame_in, (1, 0, 2))
    cache_far = jnp.transpose(conv_cache, (0, 2, 1, 3))
    gain_far = norm_gain.reshape(1, channels)

    rows = edge_rows(width)
    tiles = [(frame_far.shape, BF16), (cache_far.shape, BF16), (gain_far.shape, F32)]
    far_tiles = (frame_far, cache_far, gain_far)
    edge = ((3, rows, channels), BF16)
    side = ((3, side_slots(height), channels), BF16)
    packed = ((3 * height + 8, channels), BF16)
    keys = ((count, channels), BF16)
    sems = [pltpu.SemaphoreType.DMA((3,))]
    hops = (chips - 1) // 2
    if narrow(lax.axis_size("cols")):
        with_row = ((count + 2 * rows, channels), BF16)
        frame, cache, gain, chain_a, to_partner = call(
            pack_chain_kernel, tiles + [with_row, with_row], (), far_args=far_tiles, scratch=sems
        )
        partner = moved(to_partner, twin_pairs)
        arrived_a = moved(chain_a, ring)
        arrived_b = moved(partner, ring)
        (chain_a,) = call(cut_kernel, [keys], (arrived_a,))
        (chain_b,) = call(cut_kernel, [keys], (arrived_b,))
        (mine,) = call(split_kernel, [((6 * rows + 2 * height, channels), BF16)], (cache, arrived_a, arrived_b))
        theirs = moved(mine, twin_pairs)
        top, bottom, twin, to_cross = call(
            sort_edges_kernel, [edge, edge, side, packed], (frame, cache, partner, mine, theirs)
        )
    else:
        frame, cache, gain, first_rows, last_rows = call(
            pack_rows_kernel, tiles + [edge, edge], (), far_args=far_tiles, scratch=sems
        )
        chain_a = frame_far.reshape(count, channels)
        chain_b = moved(chain_a, twin_pairs)
        chain_a = moved(chain_a, ring)
        chain_b = moved(chain_b, ring)
        top = moved(last_rows, down)
        bottom = moved(first_rows, up)
        to_twin, to_cross = call(pack_cols_kernel, [side, packed], (frame, cache, top, bottom))
        twin = moved(to_twin, twin_pairs)
    cross = moved(to_cross, cross_pairs)
    blocks = [frame, chain_a, chain_b]
    for _ in range(1, hops):
        chain_a = moved(chain_a, ring)
        chain_b = moved(chain_b, ring)
        blocks += [chain_a, chain_b]
    last_a = moved(chain_a, ring)
    last_b = moved(last_a, twin_pairs)

    far_args = (
        w_query, w_key, w_value, w_out, conv_gain.reshape(1, channels),
        conv_bias.reshape(1, out_channels), w_conv,
    )
    w_query, w_key, w_value, w_out, conv_gain, conv_bias, w_conv = far_args
    square = ((channels, channels), BF16)
    w_query_key, w_value_out = call(combine_kernel, [square, square], (w_query, w_key, w_value, w_out))
    ext = ((2 * edge_slots(width) + (width + 2) * height, channels), BF16)
    raw, queries = call(query_kernel, [ext, ext], (frame, top, bottom, twin, cross, gain, w_query_key))
    twin_queries = moved(queries, twin_pairs)
    (partial,) = call(cache_conv_kernel, [((count, out_channels), F32)], (cache, top, bottom, twin, cross, w_conv))
    states = None
    for k in range(0, len(blocks), 7):
        states = fold(states, queries, twin_queries, gain, blocks[k : k + 7], k + 7 >= len(blocks))
    other = moved(states[1], twin_pairs)
    other_scale = moved(states[2], twin_pairs)
    (state,) = call(fold_own_kernel, [(states[0].shape, F32)], (gain, queries, last_a, states[0]))
    hidden, mixed = call(
        functools.partial(finish_kernel, height),
        [((count, channels), BF16), ((count, out_channels), BF16)],
        (
            state, other, other_scale, queries, last_b, gain, raw, partial, w_value_out, conv_gain, conv_bias, w_conv,
        ),
        24 << 20,
        far=True,
    )
    hidden = jnp.transpose(hidden.reshape(width, height, channels), (1, 0, 2))
    mixed = jnp.transpose(mixed.reshape(width, height, out_channels), (1, 0, 2))
    return (hidden, mixed)


def solution(mesh):
    in_specs = (
        P(("video", "rows"), "cols", None),
        P(),
        P(),
        P(),
        P(),
        P(),
        P(),
        P(None, ("video", "rows"), "cols", None),
        P(),
        P(),
    )
    out_specs = (P(("video", "rows"), "cols", None), P(("video", "rows"), "cols", None))
    return jax.shard_map(block, mesh=mesh, in_specs=in_specs, out_specs=out_specs, check_vma=False)
```

```python
import functools
import math

import jax
import jax.numpy as jnp
from jax import lax
from jax.experimental import pallas as pl
from jax.experimental.pallas import tpu as pltpu
from jax.sharding import PartitionSpec as P


EPS = 1e-06
AXES = ("rows", "cols")
F32 = jnp.float32
COST = 2_000_000_000
BF16 = jnp.bfloat16
VM = pl.BlockSpec(memory_space=pltpu.VMEM)


def near(value):
    return pltpu.with_memory_space_constraint(value, pltpu.VMEM)


def call(kernel, outs, args, limit=16 << 20, far_args=(), far=False, scratch=()):
    return pl.pallas_call(
        kernel,
        in_specs=[VM] * len(args) + [pl.BlockSpec(memory_space=pltpu.HBM)] * len(far_args),
        out_specs=[VM] * len(outs),
        out_shape=[
            jax.ShapeDtypeStruct(shape, dtype) if far else pltpu.VMEM(shape, dtype)
            for shape, dtype in outs
        ],
        scratch_shapes=scratch,
        compiler_params=pltpu.CompilerParams(vmem_limit_bytes=limit),
        cost_estimate=pl.CostEstimate(flops=COST, bytes_accessed=4 << 20, transcendentals=0),
    )(*[near(a) for a in args], *[pltpu.with_memory_space_constraint(a, pltpu.HBM) for a in far_args])


def chip_cycle(height, width):
    if width == 1 or height == 1:
        return [(z, x) for z in range(height) for x in range(width)]
    order = []
    for x in range(width):
        inner = range(1, height) if x % 2 == 0 else range(height - 1, 0, -1)
        order += [(z, x) for z in inner]
    return order + [(0, x) for x in range(width - 1, -1, -1)]


def permutations(rows, cols):
    def at(z, x, core):
        return z * cols + 2 * x + core

    walk = chip_cycle(rows, cols // 2)
    ring = []
    for k, here in enumerate(walk):
        there = walk[(k + 1) % len(walk)]
        ring += [(at(*here, 0), at(*there, 0)), (at(*there, 1), at(*here, 1))]
    twin = [(i, i ^ 1) for i in range(rows * cols)]
    down = [(i, i + cols) for i in range((rows - 1) * cols)]
    up = [(j, i) for i, j in down]
    cross = []
    for r in range(rows):
        for c in range(1, cols - 1, 2):
            i = r * cols + c
            cross += [(i, i + 1), (i + 1, i)]
    return len(walk), ring, twin, down, up, cross


def edge_slots(width):
    return -(-(width + 2) // 8) * 8


def edge_rows(width):
    return -(-width // 8) * 8


def side_slots(height):
    return height + 8


def rms_scaled(values, gain):
    mean_sq = jnp.mean(values * values, axis=-1, keepdims=True)
    return values * lax.rsqrt(mean_sq + EPS) * gain


def dot(a, b):
    return jnp.dot(a, b, preferred_element_type=F32)


def dot_t(a, b):
    return lax.dot_general(a, b, (((1,), (1,)), ((), ())), preferred_element_type=F32)


def row_edge(tile, r):
    width, _, channels = tile.shape
    fill = jnp.zeros((edge_rows(width) - width, channels), F32)
    return jnp.concatenate([tile[c, r : r + 1, :] for c in range(width)] + [fill], axis=0)


def load_tiles(frame_hbm, cache_hbm, gain_hbm, frame_ref, cache_ref, gain_ref, sems):
    copies = [
        pltpu.make_async_copy(frame_hbm, frame_ref, sems.at[0]),
        pltpu.make_async_copy(cache_hbm, cache_ref, sems.at[1]),
        pltpu.make_async_copy(gain_hbm, gain_ref, sems.at[2]),
    ]
    for copy in copies:
        copy.start()
    for copy in copies:
        copy.wait()


def pack_rows_kernel(frame_hbm, cache_hbm, gain_hbm, frame_ref, cache_ref, gain_ref, first_ref, last_ref, sems):
    load_tiles(frame_hbm, cache_hbm, gain_hbm, frame_ref, cache_ref, gain_ref, sems)
    height = frame_ref.shape[1]
    for t in range(3):
        tile = (frame_ref[...] if t == 2 else cache_ref[t]).astype(F32)
        first_ref[t] = row_edge(tile, 0).astype(BF16)
        last_ref[t] = row_edge(tile, height - 1).astype(BF16)


def faces_up():
    col = lax.axis_index("cols")
    return lax.rem(lax.rem(col, 2) + lax.div(col, 2), 2)


def pack_chain_kernel(frame_hbm, cache_hbm, gain_hbm, frame_ref, cache_ref, gain_ref, chain_ref, swap_ref, sems):
    load_tiles(frame_hbm, cache_hbm, gain_hbm, frame_ref, cache_ref, gain_ref, sems)
    width, height, channels = frame_ref.shape
    count, rows = width * height, edge_rows(width)
    up = faces_up()
    chain_ref[:count] = frame_ref[...].reshape(count, channels)
    swap_ref[:count] = frame_ref[...].reshape(count, channels)
    for t in range(2):
        tile = cache_ref[t].astype(F32)
        first, last = row_edge(tile, 0), row_edge(tile, height - 1)
        at = count + t * rows
        chain_ref[at : at + rows] = jnp.where(up == 1, first, last).astype(BF16)
        swap_ref[at : at + rows] = jnp.where(up == 1, last, first).astype(BF16)


def cut_kernel(arrived_ref, chain_ref):
    chain_ref[...] = arrived_ref[: chain_ref.shape[0]]


def split_kernel(cache_ref, a_ref, b_ref, edges_ref):
    _, width, height, _ = cache_ref.shape
    count, rows = width * height, edge_rows(width)
    up = faces_up()
    odd = lax.rem(lax.axis_index("cols"), 2)
    for k, ref in enumerate((a_ref, b_ref)):
        to = k * 3 * rows
        edges_ref[to : to + 2 * rows] = ref[count : count + 2 * rows]
        tile = ref[:count].astype(F32).reshape(width, height, -1)
        edge = jnp.where(up == 1, row_edge(tile, 0), row_edge(tile, height - 1))
        edges_ref[to + 2 * rows : to + 3 * rows] = edge.astype(BF16)
    for t in range(2):
        at = 6 * rows + t * height
        column = jnp.where(odd == 1, cache_ref[t, 0].astype(F32), cache_ref[t, width - 1].astype(F32))
        edges_ref[at : at + height] = column.astype(BF16)


def sort_edges_kernel(
    frame_ref, cache_ref, partner_ref, mine_ref, theirs_ref, top_ref, bottom_ref, twin_ref, cross_ref
):
    width, height, channels = frame_ref.shape
    count, rows = width * height, top_ref.shape[1]
    up = faces_up()
    odd = lax.rem(lax.axis_index("cols"), 2)
    row = lax.axis_index("rows")
    has_top, has_bottom = row > 0, row < lax.axis_size("rows") - 1
    fill = jnp.zeros((side_slots(height) - height - 2, channels), F32)
    columns, ends = [], []
    for t in range(3):
        pair = []
        for k in range(2):
            mine = mine_ref[(3 * k + t) * rows : (3 * k + t + 1) * rows].astype(F32)
            theirs = theirs_ref[(3 - 3 * k + t) * rows : (4 - 3 * k + t) * rows].astype(F32)
            top = jnp.where(has_top, jnp.where(up == 1, theirs, mine), 0.0)
            bottom = jnp.where(has_bottom, jnp.where(up == 1, mine, theirs), 0.0)
            pair.append((top, bottom))
        (top, bottom), (twin_top, twin_bottom) = pair
        top_ref[t] = top.astype(BF16)
        bottom_ref[t] = bottom.astype(BF16)

        def facing(first, value, axis_rows):
            a, b = value[axis_rows(0)], value[axis_rows(width - 1)]
            return jnp.where(first, a, b)

        if t == 2:
            block = partner_ref[:count].astype(F32)
            column = facing(odd == 0, block, lambda c: slice(c * height, (c + 1) * height))
        else:
            at = 6 * rows + t * height
            column = theirs_ref[at : at + height].astype(F32)
        corners = [facing(odd == 0, v, lambda c: slice(c, c + 1)) for v in (twin_top, twin_bottom)]
        twin_ref[t] = jnp.concatenate([column, *corners, fill], axis=0).astype(BF16)
        tile = (frame_ref[...] if t == 2 else cache_ref[t]).astype(F32)
        column = jnp.where(odd == 0, tile[0], tile[width - 1])
        corners = [facing(odd == 0, v, lambda c: slice(c, c + 1)) for v in (top, bottom)]
        columns.append(column)
        ends += corners
    cross_ref[...] = to_side(columns, ends)


def pack_cols_kernel(frame_ref, cache_ref, top_ref, bottom_ref, twin_ref, cross_ref):
    width, height, channels = frame_ref.shape
    odd = lax.rem(lax.axis_index("cols"), 2)
    fill = jnp.zeros((side_slots(height) - height - 2, channels), F32)
    columns, ends = [], []
    for t in range(3):
        sides = []
        for c in (0, width - 1):
            own = (frame_ref[c] if t == 2 else cache_ref[t, c]).astype(F32)
            top = top_ref[t].astype(F32)[c : c + 1, :]
            bottom = bottom_ref[t].astype(F32)[c : c + 1, :]
            sides.append(jnp.concatenate([own, top, bottom, fill], axis=0))
        left, right = sides
        twin_ref[t] = jnp.where(odd == 1, left, right).astype(BF16)
        side = jnp.where(odd == 1, right, left)
        columns.append(side[:height])
        ends.append(side[height : height + 2])
    cross_ref[...] = to_side(columns, [e[k : k + 1] for e in ends for k in range(2)])


def extended(own, top, bottom, twin, cross, odd):
    height = twin.shape[0] - side_slots(0)
    left = jnp.where(odd == 1, twin, cross)
    right = jnp.where(odd == 1, cross, twin)
    width = own.shape[0] // height
    slots = edge_slots(width)
    slot = lax.broadcasted_iota(jnp.int32, (slots, own.shape[1]), 0)
    spare = slots - top.shape[0]

    def edge(row, k):
        if spare:
            row = jnp.concatenate([row, jnp.zeros((spare, own.shape[1]), F32)], axis=0)
        row = jnp.where(slot == width, right[k : k + 1, :], row)
        return jnp.where(slot == slots - 1, left[k : k + 1, :], row)

    return jnp.concatenate(
        [edge(top, height), left[:height], own, right[:height], edge(bottom, height + 1)], axis=0
    )


def from_side(ref, t):
    height = (ref.shape[0] - 8) // 3
    side = ref[...].astype(F32)
    fill = jnp.zeros((side_slots(height) - height - 2, side.shape[1]), F32)
    at = 3 * height + 2 * t
    return jnp.concatenate([side[t * height : (t + 1) * height], side[at : at + 2], fill], axis=0)


def to_side(columns, corners):
    fill = jnp.zeros((8 - len(corners), corners[0].shape[1]), F32)
    return jnp.concatenate([*columns, *corners, fill], axis=0).astype(BF16)


def tap_rows(tokens, height, count):
    slots = edge_slots(count // height)
    main = tokens[slots : tokens.shape[0] - slots]
    mains = [main[j * height : j * height + count] for j in range(3)]
    result = []
    for edge in (tokens[:slots], None, tokens[tokens.shape[0] - slots :]):
        if edge is None:
            parts = mains
        else:
            edges = [pltpu.roll(edge, 1, 0), edge, pltpu.roll(edge, slots - 1, 0)]
            parts = [jnp.concatenate(pair, axis=0) for pair in zip(mains, edges)]
        result.append(jnp.concatenate([p.astype(BF16) for p in parts], axis=1))
    return result


def shifted_rows(sums, i, height, count):
    if i == 1:
        return sums
    main, edge = sums[:count], sums[count:]
    out = main.shape[1]
    width = count // height
    tile = main.reshape(width, height, out)
    moved = pltpu.roll(tile, 1 if i == 0 else height - 1, 1)
    row = lax.broadcasted_iota(jnp.int32, (height, out), 0)
    at = 0 if i == 0 else height - 1
    cells = [jnp.where(row == at, edge[c : c + 1, :], moved[c]) for c in range(width)]
    return jnp.concatenate(cells, axis=0)


def cache_conv_kernel(cache_ref, top_ref, bottom_ref, twin_ref, cross_ref, w_ref, out_ref):
    width, height, channels = cache_ref.shape[1:]
    count = width * height
    odd = lax.rem(lax.axis_index("cols"), 2)
    rows = [
        tap_rows(
            extended(
                cache_ref[t].reshape(count, channels).astype(F32),
                top_ref[t].astype(F32),
                bottom_ref[t].astype(F32),
                twin_ref[t].astype(F32),
                from_side(cross_ref, t),
                odd,
            ),
            height,
            count,
        )
        for t in range(2)
    ]
    result = None
    for i in range(3):
        patches = jnp.concatenate([rows[0][i], rows[1][i]], axis=1)
        taps = w_ref[:2, i].reshape(-1, w_ref.shape[4])
        value = shifted_rows(dot(patches, taps), i, height, count)
        result = value if result is None else result + value
    out_ref[...] = result


def query_kernel(
    frame_ref, top_ref, bottom_ref, twin_ref, cross_ref, gain_ref, wqk_ref, raw_ref, keys_ref
):
    width, height, channels = frame_ref.shape
    odd = lax.rem(lax.axis_index("cols"), 2)
    tokens = extended(
        frame_ref[...].reshape(width * height, channels).astype(F32),
        top_ref[2].astype(F32),
        bottom_ref[2].astype(F32),
        twin_ref[2].astype(F32),
        from_side(cross_ref, 2),
        odd,
    )
    raw_ref[...] = tokens.astype(BF16)
    normed = rms_scaled(tokens, gain_ref[...]).astype(BF16)
    keys_ref[...] = (dot(normed, wqk_ref[...]) * (1.0 / math.sqrt(channels))).astype(BF16)


def lanes(value, width):
    return jnp.broadcast_to(value, (value.shape[0], width))


def key_rows(refs, gain, ready=()):
    parts = [ref[...] for ref in ready] + [
        rms_scaled(ref[...].reshape(-1, gain.shape[1]).astype(F32), gain).astype(BF16) for ref in refs
    ]
    return parts[0] if len(parts) == 1 else jnp.concatenate(parts, axis=0)


def norm_kernel(gain_ref, *refs):
    refs[-1][...] = key_rows(refs[:-1], gain_ref[...])


def fold_kernel(blocks, ready, first, last, gain_ref, own_ref, twin_ref, *refs):
    keys = key_rows(refs[ready:blocks], gain_ref[...], refs[:ready])
    refs = refs[blocks:]
    states, outs = ((None, None), refs) if first else (refs[:2], refs[2:])
    channels = keys.shape[1]
    length = own_ref.shape[0]
    all_scores = dot_t(jnp.concatenate([own_ref[...], twin_ref[...]], axis=0), keys)
    peaks, totals, weights = [], [], []
    for k, state in enumerate(states):
        scores = all_scores[k * length : (k + 1) * length]
        peak = jnp.max(scores, axis=1, keepdims=True)
        if not first:
            peak = jnp.maximum(peak, state[:, channels : channels + 1])
        part = jnp.exp(scores - peak)
        peaks.append(peak)
        totals.append(jnp.sum(part, axis=1, keepdims=True))
        weights.append(part.astype(BF16))
    all_summed = dot(jnp.concatenate(weights, axis=0), keys)
    for k, (state, out) in enumerate(zip(states, outs)):
        summed, total, peak = all_summed[k * length : (k + 1) * length], totals[k], peaks[k]
        if not first:
            fade = jnp.exp(state[:, channels : channels + 1] - peak)
            total = total + fade * state[:, channels + 128 : channels + 129]
            summed = summed + fade * state[:, :channels]
        if last and k == 1:
            out[...] = summed.astype(BF16)
            outs[2][:, :128] = lanes(peak, 128)
            outs[2][:, 128:] = lanes(total, 128)
        else:
            out[:, :channels] = summed
            out[:, channels : channels + 128] = lanes(peak, 128)
            out[:, channels + 128 :] = lanes(total, 128)


def fold(states, own, twin, gain, blocks, ready, last):
    length, channels = own.shape
    shape = ((length, channels + 256), F32)
    first = states is None
    args = (gain, own, twin, *blocks, *(() if first else states))
    kernel = functools.partial(fold_kernel, len(blocks), ready, first, last)
    others = [((length, channels), BF16), ((length, 256), F32)] if last else [shape]
    return call(kernel, [shape, *others], args, 24 << 20)


def spread(column, width):
    return jnp.concatenate([column] * -(-width // 128), axis=1)[:, :width]


def fold_own_kernel(gain_ref, query_ref, block_ref, state_ref, out_ref):
    keys = key_rows((block_ref,), gain_ref[...])
    channels = keys.shape[1]
    scores = dot_t(query_ref[...], keys)
    before = state_ref[:, channels : channels + 128]
    peak = jnp.maximum(before, lanes(jnp.max(scores, axis=1, keepdims=True), 128))
    fade = jnp.exp(before - peak)
    weights = jnp.exp(scores - spread(peak, scores.shape[1]))
    total = lanes(jnp.sum(weights, axis=1, keepdims=True), 128)
    summed = dot(weights.astype(BF16), keys)
    out_ref[:, :channels] = summed + spread(fade, channels) * state_ref[:, :channels]
    out_ref[:, channels : channels + 128] = peak
    out_ref[:, channels + 128 :] = total + fade * state_ref[:, channels + 128 :]


def combine_kernel(wq_ref, wk_ref, wv_ref, wo_ref, query_key_ref, value_out_ref):
    query_key_ref[...] = dot_t(wq_ref[...], wk_ref[...]).astype(BF16)
    value_out_ref[...] = dot(wv_ref[...], wo_ref[...]).astype(BF16)


def finish_kernel(
    height, state_ref, other_ref, scale_ref, query_ref, last_ref, key_gain_ref, raw_ref, partial_ref,
    wvo_ref, gain_ref, bias_ref, w_ref, hidden_ref, mixed_ref,
):
    length, channels = raw_ref.shape
    count, out = partial_ref.shape
    slots = edge_slots(count // height)
    row = lax.axis_index("rows")
    col = lax.axis_index("cols")
    has_top, has_bottom = row > 0, row < lax.axis_size("rows") - 1
    has_left, has_right = col > 0, col < lax.axis_size("cols") - 1

    keys = key_rows((last_ref,), key_gain_ref[...])
    scores = dot_t(query_ref[...], keys)
    peak_a, total_a = state_ref[:, channels : channels + 128], state_ref[:, channels + 128 :]
    peak_b, total_b = scale_ref[:, :128], scale_ref[:, 128:]
    peak = jnp.maximum(peak_a, peak_b)
    peak = jnp.maximum(peak, lanes(jnp.max(scores, axis=1, keepdims=True), 128))
    fade_a, fade_b = jnp.exp(peak_a - peak), jnp.exp(peak_b - peak)
    weights = jnp.exp(scores - spread(peak, scores.shape[1]))
    total = lanes(jnp.sum(weights, axis=1, keepdims=True), 128)
    total = total + fade_a * total_a + fade_b * total_b
    summed = dot(weights.astype(BF16), keys)
    summed = summed + spread(fade_a, channels) * state_ref[:, :channels]
    summed = summed + spread(fade_b, channels) * other_ref[...].astype(F32)
    pooled = (summed * spread(1.0 / total, channels)).astype(BF16)
    hidden = (raw_ref[...].astype(F32) + dot(pooled, wvo_ref[...])).astype(BF16)
    wide = hidden.astype(F32)
    value = rms_scaled(wide, gain_ref[...])
    value = value / (1.0 + jnp.exp(-value))
    slot = lax.broadcasted_iota(jnp.int32, (length, 1), 0)
    main_end = length - slots
    width = count // height
    in_top, in_bottom = slot < slots, slot >= main_end
    in_left = (slot >= slots) & (slot < slots + height)
    in_right = (slot >= main_end - height) & (slot < main_end)
    in_left = in_left | (slot == slots - 1) | (slot == length - 1)
    in_right = in_right | (slot == width) | (slot == main_end + width)
    outside = (in_top & jnp.logical_not(has_top)) | (in_bottom & jnp.logical_not(has_bottom))
    outside = outside | (in_left & jnp.logical_not(has_left)) | (in_right & jnp.logical_not(has_right))
    rows = tap_rows(jnp.where(outside, 0.0, value), height, count)

    own = hidden[slots + height : slots + height + count]
    hidden_ref[...] = own
    result = partial_ref[...] + own[:, :out].astype(F32) + bias_ref[...]
    for i in range(3):
        taps = w_ref[2, i].reshape(-1, out)
        result = result + shifted_rows(dot(rows[i], taps), i, height, count)
    mixed_ref[...] = result.astype(BF16)


def narrow(cols):
    return cols == 4


def moved(value, pairs):
    return lax.ppermute(value, AXES, pairs)


def block(
    frame_in, norm_gain, w_query, w_key, w_value, w_out, conv_gain, conv_cache, w_conv, conv_bias
):
    height, width, channels = frame_in.shape
    out_channels = w_conv.shape[4]
    count = height * width
    chips, ring, twin_pairs, down, up, cross_pairs = permutations(
        lax.axis_size("rows"), lax.axis_size("cols")
    )
    frame_far = jnp.transpose(frame_in, (1, 0, 2))
    cache_far = jnp.transpose(conv_cache, (0, 2, 1, 3))
    gain_far = norm_gain.reshape(1, channels)

    rows = edge_rows(width)
    tiles = [(frame_far.shape, BF16), (cache_far.shape, BF16), (gain_far.shape, F32)]
    far_tiles = (frame_far, cache_far, gain_far)
    edge = ((3, rows, channels), BF16)
    side = ((3, side_slots(height), channels), BF16)
    packed = ((3 * height + 8, channels), BF16)
    keys = ((count, channels), BF16)
    sems = [pltpu.SemaphoreType.DMA((3,))]
    hops = (chips - 1) // 2
    if narrow(lax.axis_size("cols")):
        with_row = ((count + 2 * rows, channels), BF16)
        frame, cache, gain, chain_a, to_partner = call(
            pack_chain_kernel, tiles + [with_row, with_row], (), far_args=far_tiles, scratch=sems
        )
        partner = moved(to_partner, twin_pairs)
        arrived_a = moved(chain_a, ring)
        arrived_b = moved(partner, ring)
        (chain_a,) = call(cut_kernel, [keys], (arrived_a,))
        (chain_b,) = call(cut_kernel, [keys], (arrived_b,))
        (mine,) = call(split_kernel, [((6 * rows + 2 * height, channels), BF16)], (cache, arrived_a, arrived_b))
        theirs = moved(mine, twin_pairs)
        top, bottom, twin, to_cross = call(
            sort_edges_kernel, [edge, edge, side, packed], (frame, cache, partner, mine, theirs)
        )
    else:
        frame, cache, gain, first_rows, last_rows = call(
            pack_rows_kernel, tiles + [edge, edge], (), far_args=far_tiles, scratch=sems
        )
        chain_a = frame_far.reshape(count, channels)
        chain_b = moved(chain_a, twin_pairs)
        chain_a = moved(chain_a, ring)
        chain_b = moved(chain_b, ring)
        top = moved(last_rows, down)
        bottom = moved(first_rows, up)
        to_twin, to_cross = call(pack_cols_kernel, [side, packed], (frame, cache, top, bottom))
        twin = moved(to_twin, twin_pairs)
    cross = moved(to_cross, cross_pairs)
    blocks = [frame, chain_a, chain_b]
    for _ in range(1, hops):
        chain_a = moved(chain_a, ring)
        chain_b = moved(chain_b, ring)
        blocks += [chain_a, chain_b]
    last_a = moved(chain_a, ring)
    last_b = moved(last_a, twin_pairs)

    far_args = (
        w_query, w_key, w_value, w_out, conv_gain.reshape(1, channels),
        conv_bias.reshape(1, out_channels), w_conv,
    )
    w_query, w_key, w_value, w_out, conv_gain, conv_bias, w_conv = far_args
    square = ((channels, channels), BF16)
    w_query_key, w_value_out = call(combine_kernel, [square, square], (w_query, w_key, w_value, w_out))
    ext = ((2 * edge_slots(width) + (width + 2) * height, channels), BF16)
    raw, queries = call(query_kernel, [ext, ext], (frame, top, bottom, twin, cross, gain, w_query_key))
    twin_queries = moved(queries, twin_pairs)
    (partial,) = call(cache_conv_kernel, [((count, out_channels), F32)], (cache, top, bottom, twin, cross, w_conv))
    states = None
    ready = 0
    if len(blocks) <= 7:
        early = blocks[:-2]
        shape = ((len(early) * count, channels), BF16)
        blocks = [*call(norm_kernel, [shape], (gain, *early)), *blocks[-2:]]
        ready = 1
    for k in range(0, len(blocks), 7):
        states = fold(states, queries, twin_queries, gain, blocks[k : k + 7], ready, k + 7 >= len(blocks))
    other = moved(states[1], twin_pairs)
    other_scale = moved(states[2], twin_pairs)
    (state,) = call(fold_own_kernel, [(states[0].shape, F32)], (gain, queries, last_a, states[0]))
    hidden, mixed = call(
        functools.partial(finish_kernel, height),
        [((count, channels), BF16), ((count, out_channels), BF16)],
        (
            state, other, other_scale, queries, last_b, gain, raw, partial, w_value_out, conv_gain, conv_bias, w_conv,
        ),
        24 << 20,
        far=True,
    )
    hidden = jnp.transpose(hidden.reshape(width, height, channels), (1, 0, 2))
    mixed = jnp.transpose(mixed.reshape(width, height, out_channels), (1, 0, 2))
    return (hidden, mixed)


def solution(mesh):
    in_specs = (
        P(("video", "rows"), "cols", None),
        P(),
        P(),
        P(),
        P(),
        P(),
        P(),
        P(None, ("video", "rows"), "cols", None),
        P(),
        P(),
    )
    out_specs = (P(("video", "rows"), "cols", None), P(("video", "rows"), "cols", None))
    return jax.shard_map(block, mesh=mesh, in_specs=in_specs, out_specs=out_specs, check_vma=False)
```
